128 devices in a mesh: row: 8 (over y_hi, x), col: 16 (over z, y_lo, core).
Axes of the slice: x: 4, y: 4 (y_hi: 2, y_lo: 2; y = y_hi * 2 + y_lo), z: 4, core: 2. Of those that a mesh axis runs over, the one named last changes fastest.
Arguments:
- features: bfloat16 [64, 1024, 1024], P(None, 'col', 'row'), may hold values from -120 to 120
- conv_first: bfloat16 [9, 64, 64], replicated, may hold values from -0.25 to 0.25
- conv_second: bfloat16 [9, 64, 64], replicated, may hold values from -0.25 to 0.25
- head_weight: bfloat16 [37, 64], replicated, may hold values from -0.75 to 0.75
- head_bias: float32 [37], replicated, may hold values from -4 to 4
- cotangent: bfloat16 [37, 1024, 1024], P(None, 'col', 'row'), may hold values from -6 to 6
Outputs:
- logits: bfloat16 [37, 1024, 1024], P(None, 'col', 'row')
- input_grad: bfloat16 [64, 1024, 1024], P(None, 'col', 'row')
- grad_first: float32 [9, 64, 64], replicated
- grad_second: float32 [9, 64, 64], replicated
- grad_head: float32 [37, 64], replicated
- grad_bias: float32 [37], replicated
The draws below stay inside these ranges and needn't reach their ends.
All inputs are finite; a program needn't handle non-finite values.
Results may differ from the reference program's by a relative error of at most 0.007.
Values may be sent and summed in bfloat16 or wider, within the bound.
No kernel may reach another device: no remote copies, remote signals or barrier semaphores. Data moves between devices by JAX's collectives and lax.ppermute only.
A program may use at most 128 MiB of HBM per device.

```python
import jax
import jax.numpy as jnp
from jax import lax

C = 64
NB = 37
DILATION_STEP = 16
L = 1024


def draw_features(key, part):
    subkeys = jax.random.split(key, 3)
    position = jnp.arange(L, dtype=jnp.float32) / L
    row_scale = jnp.exp(jax.random.uniform(subkeys[1], (L,), minval=-1.15, maxval=1.15) + 0.55 * (2.0 * position - 1.0))
    col_scale = jnp.exp(jax.random.uniform(subkeys[2], (L,), minval=-1.15, maxval=1.15) + 0.3 * (2.0 * position - 1.0))
    baseline = jax.random.normal(subkeys[0], (C, L, L))
    baseline = jnp.clip(baseline, -5.0, 5.0)
    return (baseline * col_scale[None, :, None] * row_scale[None, None, :]).astype(jnp.bfloat16)


def block_scale(key, dims, shards, least, largest):
    def one(dim, blocks):
        steps = jax.random.uniform(jax.random.fold_in(jax.random.fold_in(key, 6), dim), (blocks,), jnp.float32, least / len(shards), largest / len(shards))
        return jnp.repeat(jnp.exp(steps), dims[dim] // blocks).reshape((-1,) + (1,) * (len(dims) - dim - 1))

    gain = one(*shards[0])
    for cut in shards[1:]:
        gain = gain * one(*cut)
    return gain


def scatter_about(stream_key, shape, scale, most, cuts=(), held_as=jnp.bfloat16):
    gain = block_scale(stream_key, shape, cuts, -0.22, 0.18) if cuts else 1.0
    array = jax.random.normal(stream_key, shape, jnp.float32) * scale * gain
    return jnp.minimum(jnp.maximum(array, -most), most).astype(held_as)


def setup_inputs(seed: int = 0) -> dict:
    key_of = jax.random.split(jax.random.key(seed), 7)
    return {
        "features": draw_features(jax.random.fold_in(key_of[6], 71), 0),
        "conv_first": scatter_about(key_of[1], (9, C, C), (9 * C) ** -0.5, 0.25),
        "conv_second": scatter_about(key_of[2], (9, C, C), (9 * C) ** -0.5, 0.25),
        "head_weight": scatter_about(key_of[3], (NB, C), C ** -0.5, 0.75),
        "head_bias": scatter_about(key_of[4], (NB,), 1.0, 4.0, (), jnp.float32),
        "cotangent": scatter_about(key_of[5], (NB, L, L), 1.0, 6.0, ((1, 16), (2, 8))),
    }


epsilon = 1e-05

def elu_apply(value_entries):
    return jnp.where(value_entries > 0, value_entries, jnp.exp(jnp.minimum(value_entries, 0.0)) - 1.0)

def elu_slope(value_entries):
    return jnp.where(value_entries > 0, 1.0, jnp.exp(jnp.minimum(value_entries, 0.0)))

def widen(value_entries):
    return jnp.pad(value_entries, ((0, 0), (DILATION_STEP, DILATION_STEP), (DILATION_STEP, DILATION_STEP)))

def tap_window(padded, kernel_row, kernel_column, adjoint, col_count, row_count):
    shift_direction = -1 if adjoint else 1
    column_shift = DILATION_STEP + shift_direction * DILATION_STEP * (kernel_column - 1)
    row_shift = DILATION_STEP + shift_direction * DILATION_STEP * (kernel_row - 1)
    window = padded[:, column_shift:column_shift + col_count, row_shift:row_shift + row_count]
    return window.reshape(padded.shape[0], col_count * row_count)

def convolve(padded, weights, col_count, row_count, adjoint):
    running = jnp.zeros((weights.shape[1], col_count * row_count), jnp.float32)
    for kernel_row in range(3):
        for kernel_column in range(3):
            window = tap_window(padded, kernel_row, kernel_column, adjoint, col_count, row_count)
            matrix = weights[3 * kernel_row + kernel_column]
            if adjoint:
                matrix = matrix.T
            running = running + jnp.dot(matrix, window, preferred_element_type=jnp.float32)
    return running.reshape(-1, col_count, row_count)

def weight_terms(gradient, padded, col_count, row_count):
    flattened = gradient.reshape(gradient.shape[0], -1)
    collected = []
    for kernel_row in range(3):
        for kernel_column in range(3):
            window = tap_window(padded, kernel_row, kernel_column, False, col_count, row_count)
            collected.append(lax.dot_general(flattened, window, (((1,), (1,)), ((), ())), preferred_element_type=jnp.float32))
    return jnp.stack(collected, 0)

def normalize(activation):
    cell_count = activation.shape[1] * activation.shape[2]
    average = lax.optimization_barrier(jnp.sum(activation, axis=(1, 2))) / cell_count
    centered = activation - average[:, None, None]
    spread = lax.optimization_barrier(jnp.sum(centered * centered, axis=(1, 2))) / cell_count
    inverse_std = lax.rsqrt(spread + epsilon)
    return (centered * inverse_std[:, None, None], inverse_std)

def norm_back(gradient, normed, inverse_std):
    cell_count = gradient.shape[1] * gradient.shape[2]
    first_mean = lax.optimization_barrier(jnp.sum(gradient, axis=(1, 2))) / cell_count
    second_mean = lax.optimization_barrier(jnp.sum(gradient * normed, axis=(1, 2))) / cell_count
    return inverse_std[:, None, None] * (gradient - first_mean[:, None, None] - normed * second_mean[:, None, None])

def reference(features, conv_first, conv_second, head_weight, head_bias, cotangent):
    channels, col_count, row_count = features.shape
    length = col_count
    wide_in = widen(features)
    act_first = convolve(wide_in, conv_first, col_count, row_count, False)
    normed_first, inverse_first = normalize(act_first)
    hidden_first = elu_apply(normed_first).astype(jnp.bfloat16)
    wide_hidden = widen(hidden_first)
    act_second = convolve(wide_hidden, conv_second, col_count, row_count, False)
    normed_second, inverse_second = normalize(act_second)
    summed = normed_second + features.astype(jnp.float32)
    hidden = elu_apply(summed).astype(jnp.bfloat16)
    flat_hidden = hidden.reshape(channels, -1)
    raw_logits = (jnp.dot(head_weight, flat_hidden, preferred_element_type=jnp.float32) + head_bias[:, None]).reshape(-1, col_count, row_count)
    logits = (0.5 * (raw_logits + jnp.swapaxes(raw_logits, 1, 2))).astype(jnp.bfloat16)
    cot_wide = cotangent.astype(jnp.float32)
    grad_sym = (0.5 * (cot_wide + jnp.swapaxes(cot_wide, 1, 2))).astype(jnp.bfloat16)
    flat_sym = grad_sym.reshape(grad_sym.shape[0], -1)
    bias_term = lax.optimization_barrier(jnp.sum(flat_sym, axis=1, dtype=jnp.float32))
    head_term = lax.dot_general(flat_sym, flat_hidden, (((1,), (1,)), ((), ())), preferred_element_type=jnp.float32)
    grad_hidden = jnp.dot(head_weight.T, flat_sym, preferred_element_type=jnp.float32).reshape(channels, col_count, row_count)
    grad_summed = grad_hidden * elu_slope(summed)
    grad_act_second = norm_back(grad_summed, normed_second, inverse_second).astype(jnp.bfloat16)
    second_term = weight_terms(grad_act_second, wide_hidden, col_count, row_count)
    grad_hidden_first = convolve(widen(grad_act_second), conv_second, col_count, row_count, True)
    grad_normed_first = grad_hidden_first * elu_slope(normed_first)
    grad_act_first = norm_back(grad_normed_first, normed_first, inverse_first).astype(jnp.bfloat16)
    first_term = weight_terms(grad_act_first, wide_in, col_count, row_count)
    input_grad = (convolve(widen(grad_act_first), conv_first, col_count, row_count, True) + grad_summed).astype(jnp.bfloat16)
    inverse_len = 1.0 / length
    return (logits, input_grad, first_term * inverse_len, second_term * inverse_len, head_term * inverse_len, bias_term * inverse_len)
```

```python
import jax
import jax.numpy as jnp
from jax import lax
from jax.sharding import PartitionSpec as P

DILATION_STEP = 16


epsilon = 1e-05


def with_halo(block, sides, width):
    for axis, dim in sides:
        count = lax.axis_size(axis)
        forward = [(i, i + 1) for i in range(count - 1)]
        backward = [(target, source) for source, target in forward]
        low = lax.ppermute(
            lax.slice_in_dim(block, block.shape[dim] - width, None, axis=dim), axis, forward
        )
        high = lax.ppermute(lax.slice_in_dim(block, 0, width, axis=dim), axis, backward)
        block = jnp.concatenate([low, block, high], axis=dim)
    return block


def elu_apply(value_entries):
    return jnp.where(
        value_entries > 0, value_entries, jnp.exp(jnp.minimum(value_entries, 0.0)) - 1.0
    )


def elu_slope(value_entries):
    return jnp.where(value_entries > 0, 1.0, jnp.exp(jnp.minimum(value_entries, 0.0)))


def widen(value_entries):
    return with_halo(value_entries, (("row", 2), ("col", 1)), DILATION_STEP)


def widen_grad(value_entries):
    return with_halo(value_entries, (("row", 2), ("col", 1)), DILATION_STEP)


def tap_window(padded, kernel_row, kernel_column, adjoint, col_count, row_count):
    shift_direction = -1 if adjoint else 1
    column_shift = DILATION_STEP + shift_direction * DILATION_STEP * (kernel_column - 1)
    row_shift = DILATION_STEP + shift_direction * DILATION_STEP * (kernel_row - 1)
    window = padded[:, column_shift : column_shift + col_count, row_shift : row_shift + row_count]
    return window.reshape(padded.shape[0], col_count * row_count)


def convolve(padded, weights, col_count, row_count, adjoint):
    running = jnp.zeros((weights.shape[1], col_count * row_count), jnp.float32)
    for kernel_row in range(3):
        for kernel_column in range(3):
            window = tap_window(padded, kernel_row, kernel_column, adjoint, col_count, row_count)
            matrix = weights[3 * kernel_row + kernel_column]
            if adjoint:
                matrix = matrix.T
            running = running + jnp.dot(matrix, window, preferred_element_type=jnp.float32)
    return running.reshape(-1, col_count, row_count)


def weight_terms(gradient, padded, col_count, row_count):
    flattened = gradient.reshape(gradient.shape[0], -1)
    collected = []
    for kernel_row in range(3):
        for kernel_column in range(3):
            window = tap_window(padded, kernel_row, kernel_column, False, col_count, row_count)
            collected.append(
                lax.dot_general(
                    flattened, window, (((1,), (1,)), ((), ())), preferred_element_type=jnp.float32
                )
            )
    return jnp.stack(collected, 0)


def share(vector):
    count = lax.axis_size("row") * lax.axis_size("col")
    spread_out = jnp.broadcast_to(vector[None], (count,) + vector.shape)
    return lax.all_to_all(spread_out, ("row", "col"), split_axis=0, concat_axis=0, tiled=True)


def total(flat, chunk):
    count = lax.axis_size("row") * lax.axis_size("col")
    padded = jnp.pad(flat, (0, count * chunk - flat.shape[0])).reshape(count, chunk)
    parts = lax.all_to_all(padded, ("row", "col"), split_axis=0, concat_axis=0, tiled=True)
    return share(jnp.sum(parts, axis=0)).reshape(-1)


def normalize(activation, cell_count):
    channels = activation.shape[0]
    own_count = activation.shape[1] * activation.shape[2]
    own_sum = jnp.sum(activation, axis=(1, 2))
    own_mean = own_sum / own_count
    off = activation - own_mean[:, None, None]
    own_square = jnp.sum(off * off, axis=(1, 2))
    table = share(jnp.concatenate([own_sum, own_square]))
    sums = table[:, :channels]
    average = jnp.sum(sums, axis=0) / cell_count
    shift = sums / own_count - average[None]
    spread = (
        jnp.sum(table[:, channels:], axis=0) + own_count * jnp.sum(shift * shift, axis=0)
    ) / cell_count
    inverse_std = lax.rsqrt(spread + epsilon)
    return ((activation - average[:, None, None]) * inverse_std[:, None, None], inverse_std)


def norm_back(gradient, normed, inverse_std, cell_count):
    channels = gradient.shape[0]
    sums = jnp.sum(
        share(
            jnp.concatenate(
                [jnp.sum(gradient, axis=(1, 2)), jnp.sum(gradient * normed, axis=(1, 2))]
            )
        ),
        axis=0,
    )
    first_mean = sums[:channels] / cell_count
    second_mean = sums[channels:] / cell_count
    return inverse_std[:, None, None] * (
        gradient - first_mean[:, None, None] - normed * second_mean[:, None, None]
    )


def mirror(tensor):
    rows = lax.axis_size("row")
    cols = lax.axis_size("col")
    ratio = cols // rows
    turned = jnp.swapaxes(tensor, 1, 2)
    planes, length, width = turned.shape
    halves = turned.reshape(planes, ratio, length // ratio, width)
    parity = lax.axis_index("col") % ratio
    got = []
    for step in range(ratio):
        half = lax.dynamic_index_in_dim(halves, (parity + step) % ratio, 1, keepdims=False)
        pairs = []
        for row in range(rows):
            for col in range(cols):
                target = (col // ratio) * cols + ratio * row + (col + step) % ratio
                pairs.append((row * cols + col, target))
        got.append(lax.ppermute(half, ("row", "col"), pairs))
    low = jnp.where(parity == 0, got[0], got[1])
    high = jnp.where(parity == 0, got[1], got[0])
    return jnp.concatenate([low, high], axis=2)


def on_device(features, conv_first, conv_second, head_weight, head_bias, cotangent):
    channels, col_count, row_count = features.shape
    length = col_count * lax.axis_size("col")
    cell_count = float(length * length)
    cot_mirror = mirror(cotangent)
    wide_in = widen(features)
    act_first = convolve(wide_in, conv_first, col_count, row_count, False)
    normed_first, inverse_first = normalize(act_first, cell_count)
    hidden_first = elu_apply(normed_first).astype(jnp.bfloat16)
    wide_hidden = widen(hidden_first)
    act_second = convolve(wide_hidden, conv_second, col_count, row_count, False)
    normed_second, inverse_second = normalize(act_second, cell_count)
    summed = normed_second + features.astype(jnp.float32)
    hidden = elu_apply(summed).astype(jnp.bfloat16)
    flat_hidden = hidden.reshape(channels, -1)
    raw_logits = (
        jnp.dot(head_weight, flat_hidden, preferred_element_type=jnp.float32) + head_bias[:, None]
    ).reshape(-1, col_count, row_count)
    logit_mirror = mirror(raw_logits.astype(jnp.bfloat16)).astype(jnp.float32)
    logits = (0.5 * (raw_logits + logit_mirror)).astype(jnp.bfloat16)
    grad_sym = (0.5 * (cotangent.astype(jnp.float32) + cot_mirror.astype(jnp.float32))).astype(
        jnp.bfloat16
    )
    flat_sym = grad_sym.reshape(grad_sym.shape[0], -1)
    bias_term = jnp.sum(flat_sym, axis=1, dtype=jnp.float32)
    head_term = lax.dot_general(
        flat_sym, flat_hidden, (((1,), (1,)), ((), ())), preferred_element_type=jnp.float32
    )
    grad_hidden = jnp.dot(head_weight.T, flat_sym, preferred_element_type=jnp.float32).reshape(
        channels, col_count, row_count
    )
    grad_summed = grad_hidden * elu_slope(summed)
    grad_act_second = norm_back(grad_summed, normed_second, inverse_second, cell_count).astype(
        jnp.bfloat16
    )
    second_term = weight_terms(grad_act_second, wide_hidden, col_count, row_count)
    grad_hidden_first = convolve(
        widen_grad(grad_act_second), conv_second, col_count, row_count, True
    )
    grad_normed_first = grad_hidden_first * elu_slope(normed_first)
    grad_act_first = norm_back(grad_normed_first, normed_first, inverse_first, cell_count).astype(
        jnp.bfloat16
    )
    first_term = weight_terms(grad_act_first, wide_in, col_count, row_count)
    input_grad = (
        convolve(widen_grad(grad_act_first), conv_first, col_count, row_count, True) + grad_summed
    ).astype(jnp.bfloat16)
    inverse_len = 1.0 / length
    early = total(jnp.concatenate([second_term.reshape(-1), head_term.reshape(-1), bias_term]), 384)
    late = total(first_term.reshape(-1), 384)
    first_size = first_term.size
    head_end = first_size + head_term.size
    return (
        logits,
        input_grad,
        (late[:first_size] * inverse_len).reshape(first_term.shape),
        (early[:first_size] * inverse_len).reshape(first_term.shape),
        (early[first_size:head_end] * inverse_len).reshape(head_term.shape),
        early[head_end : head_end + bias_term.size] * inverse_len,
    )


def solution(mesh):
    placed = (P(None, "col", "row"), P(), P(), P(), P(), P(None, "col", "row"))
    return jax.shard_map(
        on_device,
        mesh=mesh,
        in_specs=placed,
        out_specs=(P(None, "col", "row"), P(None, "col", "row"), P(), P(), P(), P()),
        check_vma=False,
    )
```

```python
import jax
import jax.numpy as jnp
from jax import lax
from jax.experimental import pallas as pl
from jax.experimental.pallas import tpu as pltpu
from jax.sharding import PartitionSpec as P


STEP = 16
GRID = 64
epsilon = 1e-05
F32 = jnp.float32
BF16 = jnp.bfloat16
ROWS = 8
COLS = 16
DEVICES = 128
CH = 64
BINS = 37
CELLS = float(1024 * 1024)
OWN = float(64 * 128)
WIDE = 24


def class_table():
    place = {}
    count = 0
    for a in range(STEP):
        for b in range(a + 1, STEP):
            place[(a, b)] = (count, 0)
            place[(b, a)] = (count, 1)
            count += 1
    for a in range(STEP // 2):
        place[(a, a)] = (count, 0)
        place[(a + 8, a + 8)] = (count, 1)
        count += 1
    return place, STEP * (STEP - 1) // 2


PLACE, FIRST_DIAGONAL = class_table()


def dot(lhs, rhs):
    return jnp.dot(lhs, rhs, preferred_element_type=F32)


def dot_nt(lhs, rhs):
    return lax.dot_general(lhs, rhs, (((1,), (1,)), ((), ())), preferred_element_type=F32)


def iota(shape, dim):
    return lax.broadcasted_iota(jnp.int32, shape, dim)


def eye(n):
    return jnp.where(iota((n, n), 0) == iota((n, n), 1), 1.0, 0.0).astype(BF16)


def class_order():
    row = iota((128, 128), 0)
    lane = iota((128, 128), 1)
    return jnp.where(lane == STEP * (row % 8) + row // 8, 1.0, 0.0).astype(BF16)


def elu(z):
    return jnp.where(z > 0, z, jnp.exp(jnp.minimum(z, 0.0)) - 1.0)


def slope(z):
    return jnp.where(z > 0, 1.0, jnp.exp(jnp.minimum(z, 0.0)))


def pack_kernel(x_ref, o_ref):
    order = class_order()
    for a in range(STEP):
        parts = []
        for h in range(2):
            x = x_ref[:, :, :] if False else jnp.concatenate(
                [x_ref[32 * h + a], x_ref[32 * h + 16 + a]], axis=0
            )
            parts.append(dot_nt(order, x))
        for b in range(STEP):
            dest, slot = PLACE[(a, b)]
            tile = jnp.concatenate([p[8 * b : 8 * b + 8] for p in parts], axis=0)
            o_ref[dest, 16 * slot : 16 * slot + 16, :] = tile.astype(BF16)


def unpack_kernel(r_ref, o_ref):
    back = class_order()
    for a in range(STEP):
        rows = [[], []]
        for b in range(STEP):
            src, slot = PLACE[(a, b)]
            tile = r_ref[src, 16 * slot : 16 * slot + 16, :].astype(F32)
            rows[0].append(tile[:8])
            rows[1].append(tile[8:])
        for h in range(2):
            z = jnp.concatenate(rows[h], axis=0)
            x = dot(z.T.astype(BF16), back).astype(BF16)
            o_ref[32 * h + a] = x[:64]
            o_ref[32 * h + 16 + a] = x[64:]


def collect(r_ref, first, put):
    unit = eye(128)

    def step(col, carry):
        rows = [[], []]
        for slot in range(2):
            for r in range(ROWS):
                tile = r_ref[r * COLS + col, first + 16 * slot : first + 16 * slot + 16, :].astype(F32)
                rows[0].append(tile[:8])
                rows[1].append(tile[8:])
        for h in range(2):
            z = jnp.concatenate(rows[h], axis=0).astype(BF16)
            t = dot_nt(unit, z)
            put(4 * col + 2 * h, t[:64])
            put(4 * col + 2 * h + 1, t[64:])
        return carry

    lax.fori_loop(0, COLS, step, 0)


def spread(o_ref, first, get):
    unit = eye(128)

    def step(col, carry):
        parts = []
        for h in range(2):
            y = jnp.concatenate([get(4 * col + 2 * h), get(4 * col + 2 * h + 1)], axis=0)
            parts.append(dot_nt(unit, y))
        for slot in range(2):
            for r in range(ROWS):
                at = 64 * slot + 8 * r
                tile = jnp.concatenate([p[at : at + 8] for p in parts], axis=0)
                o_ref[r * COLS + col, first + 16 * slot : first + 16 * slot + 16, :] = tile.astype(BF16)
        return carry

    lax.fori_loop(0, COLS, step, 0)


def put_taps(dst_ref, at, v):
    lane = iota((CH, 128), 1) % GRID
    dst_ref[at, 0:64, :] = jnp.where(lane == 0, 0.0, pltpu.roll(v, 1, 1)).astype(BF16)
    dst_ref[at, 64:128, :] = v.astype(BF16)
    dst_ref[at, 128:192, :] = jnp.where(lane == GRID - 1, 0.0, pltpu.roll(v, 127, 1)).astype(BF16)


def stack_weights(w_ref, dst_ref, adjoint):
    for kb in range(3):
        row = []
        for ka in range(3):
            if adjoint:
                row.append(w_ref[3 * (2 - ka) + (2 - kb)].astype(F32).T.astype(BF16))
            else:
                row.append(w_ref[3 * ka + kb])
        dst_ref[64 * kb : 64 * kb + 64, :] = jnp.concatenate(row, axis=1)


def convolve(w_ref, taps_ref, emit, state):
    w = w_ref[...]

    def step(t, carry):
        one, two, state = carry
        rhs = jnp.concatenate([taps_ref[2 * t], taps_ref[2 * t + 1]], axis=1)
        p = dot(w, rhs)
        a0, a1, a2 = p[0:64, :128], p[64:128, :128], p[128:192, :128]
        b0, b1, b2 = p[0:64, 128:], p[64:128, 128:], p[128:192, 128:]
        state = emit(2 * t - 1, one + a2, state)
        state = emit(2 * t, two + a1 + b2, state)
        return a0 + b1, b0, state

    zero = jnp.zeros((CH, 128), F32)
    one, two, state = lax.fori_loop(0, GRID // 2, step, (zero, zero, state))
    return emit(GRID - 1, one, state)


def weight_terms(u_ref, taps_ref, acc_ref):
    acc_ref[...] = jnp.zeros((192, 192), F32)

    def step(t, carry):
        lhs = []
        rhs = []
        for k in range(4):
            at = 4 * t + k
            lhs.append(jnp.concatenate([u_ref[at + 2], u_ref[at + 1], u_ref[at]], axis=0))
            rhs.append(taps_ref[at])
        acc_ref[...] += dot_nt(jnp.concatenate(lhs, axis=1), jnp.concatenate(rhs, axis=1))
        return carry

    lax.fori_loop(0, GRID // 4, step, 0)


def own_row(first, second):
    one = jnp.broadcast_to(jnp.sum(first, axis=1, keepdims=True), (CH, 128)).T
    two = jnp.broadcast_to(jnp.sum(second, axis=1, keepdims=True), (CH, 128)).T
    return jnp.concatenate([one[:, :64], two[:, :64]], axis=1)


def turned(row):
    return jnp.broadcast_to(row, (128, 128)).T


def moments(table_ref):
    table = table_ref[...]
    sums = jnp.sum(table, axis=0, keepdims=True)
    mean_row = sums / CELLS
    off = table / OWN - mean_row
    between = turned(OWN * jnp.sum(off * off, axis=0, keepdims=True))
    total = turned(sums)
    mean = total[:64] / CELLS
    spread_ = (total[64:] + between[:64]) / CELLS
    return mean, lax.rsqrt(spread_ + epsilon)


def means(table_ref):
    total = turned(jnp.sum(table_ref[...], axis=0, keepdims=True))
    return total[:64] / CELLS, total[64:] / CELLS


def own_moments(act_ref, total):
    mean = jnp.broadcast_to(jnp.sum(total, axis=1, keepdims=True) / OWN, (CH, 128))

    def step(j, acc):
        off = act_ref[j] - mean
        return acc + off * off

    square = lax.fori_loop(0, GRID, step, jnp.zeros((CH, 128), F32), unroll=4)
    return own_row(total, square)


def symmetric(x_ref, k_ref, flag, put):
    bins = x_ref.shape[1]
    k_ref[...] = jnp.swapaxes(x_ref[...], 0, 1)

    def step(k, carry):
        x = k_ref[k]
        t = x.T
        low, high = t[:64], t[64:]
        m = jnp.where(
            flag > 0,
            jnp.concatenate([low, high], axis=1),
            jnp.concatenate([high, low], axis=1),
        )
        k_ref[k] = 0.5 * (x + m)
        return carry

    lax.fori_loop(0, bins, step, 0, unroll=2)
    x_ref[...] = jnp.swapaxes(k_ref[...], 0, 1)


def first_kernel(flag_ref, r_ref, w_ref, act_ref, stat_ref, taps_ref, sym_ref, x_ref, k_ref, w_s):
    stack_weights(w_ref, w_s, False)

    def put(j, v):
        put_taps(taps_ref, j, v)

    collect(r_ref, 0, put)

    def emit(j, v, total):
        act_ref[jnp.maximum(j, 0)] = v
        return total + jnp.where(j >= 0, v, 0.0)

    total = convolve(w_s, taps_ref, emit, jnp.zeros((CH, 128), F32))
    stat_ref[...] = own_moments(act_ref, total)

    def put_cot(j, v):
        x_ref[j] = v[:40]

    collect(r_ref, 32, put_cot)
    symmetric(x_ref, k_ref, flag_ref[0], None)
    sym_ref[...] = x_ref[...].astype(BF16)


def second_kernel(act_ref, table_ref, w_ref, out_ref, stat_ref, taps_ref, w_s):
    stack_weights(w_ref, w_s, False)
    mean, inverse = moments(table_ref)

    def step(j, carry):
        put_taps(taps_ref, j, elu((act_ref[j] - mean) * inverse))
        return carry

    lax.fori_loop(0, GRID, step, 0, unroll=2)

    def emit(j, v, total):
        out_ref[jnp.maximum(j, 0)] = v
        return total + jnp.where(j >= 0, v, 0.0)

    total = convolve(w_s, taps_ref, emit, jnp.zeros((CH, 128), F32))
    stat_ref[...] = own_moments(out_ref, total)


def third_kernel(act_ref, table_ref, taps_ref, sym_ref, head_ref, bias_ref, grad_ref, stat_ref, raw_ref, term_ref):
    mean, inverse = moments(table_ref)
    head = head_ref[...]
    head_t = head.astype(F32).T.astype(BF16)
    bias = bias_ref[...]

    def step(j, carry):
        first, second, count, term = carry
        normed = (act_ref[j] - mean) * inverse
        summed = normed + taps_ref[j, 64:128, :].astype(F32)
        hidden = elu(summed).astype(BF16)
        sym = sym_ref[j]
        raw_ref[j] = dot(head, hidden) + bias
        grad = dot(head_t, sym) * slope(summed)
        grad_ref[j] = grad
        term = term + dot_nt(sym, hidden)
        return first + grad, second + grad * normed, count + sym.astype(F32), term

    zero = jnp.zeros((CH, 128), F32)
    first, second, count, term = lax.fori_loop(
        0, GRID, step, (zero, zero, jnp.zeros((40, 128), F32), jnp.zeros((40, 64), F32)), unroll=2
    )
    stat_ref[...] = own_row(first, second)
    count = jnp.broadcast_to(jnp.sum(count, axis=1, keepdims=True), (40, 64))
    term_ref[...] = jnp.concatenate([term, count], axis=1)


def store_terms(acc_ref, out_ref):
    acc = acc_ref[...]
    left = acc[:, :128]
    right = jnp.concatenate([acc[:96, 128:], acc[96:, 128:]], axis=1)
    out_ref[0:24] = left.reshape(24, 8, 128)
    out_ref[24:36] = right.reshape(12, 8, 128)


def fourth_kernel(
    flag_ref, act_ref, table_ref, grad_ref, table3_ref, taps_ref, act1_ref, table1_ref, w_ref, term_ref, raw_ref,
    out_ref, stat_ref, part_ref, logit_ref,
    u_ref, utaps_ref, acc_ref, w_s, k_ref, x_ref
):
    stack_weights(w_ref, w_s, True)
    mean, inverse = moments(table_ref)
    first_mean, second_mean = means(table3_ref)
    u_ref[0] = jnp.zeros((CH, 128), BF16)
    u_ref[GRID + 1] = jnp.zeros((CH, 128), BF16)

    def step(j, carry):
        normed = (act_ref[j] - mean) * inverse
        u = inverse * (grad_ref[j] - first_mean - normed * second_mean)
        u_ref[j + 1] = u.astype(BF16)
        put_taps(utaps_ref, j, u)
        return carry

    lax.fori_loop(0, GRID, step, 0, unroll=2)
    mean1, inverse1 = moments(table1_ref)

    def emit(j, v, carry):
        first, second = carry
        at = jnp.maximum(j, 0)
        normed = (act1_ref[at] - mean1) * inverse1
        grad = jnp.where(j >= 0, v * slope(normed), 0.0)
        out_ref[at] = grad
        return first + grad, second + grad * normed

    zero = jnp.zeros((CH, 128), F32)
    first, second = convolve(w_s, utaps_ref, emit, (zero, zero))
    stat_ref[...] = own_row(first, second)
    weight_terms(u_ref, taps_ref, acc_ref)
    store_terms(acc_ref, part_ref)
    part_ref[36:41] = term_ref[...].reshape(5, 8, 128)
    x_ref[...] = raw_ref[...]
    symmetric(x_ref, k_ref, flag_ref[0], None)
    logit_ref[...] = x_ref[...].astype(BF16)


def fifth_kernel(
    grad_ref, table4_ref, act1_ref, table1_ref, taps_ref, part_ref, utaps_ref, u_ref, acc_ref
):
    mean1, inverse1 = moments(table1_ref)
    first_mean, second_mean = means(table4_ref)
    u_ref[0] = jnp.zeros((CH, 128), BF16)
    u_ref[GRID + 1] = jnp.zeros((CH, 128), BF16)

    def step(j, carry):
        normed = (act1_ref[j] - mean1) * inverse1
        u = inverse1 * (grad_ref[j] - first_mean - normed * second_mean)
        u_ref[j + 1] = u.astype(BF16)
        put_taps(utaps_ref, j, u)
        return carry

    lax.fori_loop(0, GRID, step, 0, unroll=2)
    weight_terms(u_ref, taps_ref, acc_ref)
    store_terms(acc_ref, part_ref)


def sixth_kernel(utaps_ref, w_ref, grad_ref, logit_ref, out_ref, x_ref, w_s):
    stack_weights(w_ref, w_s, True)

    def emit(j, v, carry):
        at = jnp.maximum(j, 0)
        x_ref[at] = (v + grad_ref[at]).astype(BF16)
        return carry

    convolve(w_s, utaps_ref, emit, 0)
    spread(out_ref, 0, lambda j: x_ref[j])
    pad = jnp.zeros((WIDE, 128), BF16)
    spread(out_ref, 32, lambda j: jnp.concatenate([logit_ref[j], pad], axis=0))


def sum_kernel(r_ref, o_ref):
    def step(k, acc):
        return acc + r_ref[k]

    total = lax.fori_loop(1, DEVICES, step, r_ref[0], unroll=8)
    o_ref[...] = jnp.broadcast_to(total[None], o_ref.shape)


def call(kernel, outs, scratch=(), smem=0, n=0):
    specs = [pl.BlockSpec(memory_space=pltpu.SMEM)] * smem + [
        pl.BlockSpec(memory_space=pltpu.VMEM)
    ] * n
    return pl.pallas_call(
        kernel,
        out_shape=tuple(jax.ShapeDtypeStruct(s, d) for s, d in outs),
        in_specs=specs,
        out_specs=tuple(pl.BlockSpec(memory_space=pltpu.VMEM) for _ in outs),
        scratch_shapes=[pltpu.VMEM(s, d) for s, d in scratch],
    )


def exchange(x):
    return lax.all_to_all(x, ("row", "col"), split_axis=0, concat_axis=0, tiled=True)


FIELD = ((GRID, CH, 128), F32)
HALF = ((GRID, CH, 128), BF16)
TAPS = ((GRID, 192, 128), BF16)
PADDED = ((GRID + 2, CH, 128), BF16)
STAT = ((128, 128), F32)
STACK = ((192, 192), BF16)
ACC = ((192, 192), F32)
PART = ((DEVICES, 8, 128), F32)
BINF = ((GRID, 40, 128), F32)
BINH = ((GRID, 40, 128), BF16)
BINK = ((40, GRID, 128), F32)


def terms_of(part):
    left = part[0:24].reshape(192, 128)
    right = part[24:36].reshape(96, 128)
    right = jnp.concatenate([right[:, :64], right[:, 64:]], axis=0)
    acc = jnp.concatenate([left, right], axis=1)
    return acc.reshape(3, CH, 3, CH).transpose(2, 0, 1, 3).reshape(9, CH, CH)


def on_device(features, conv_first, conv_second, head_weight, head_bias, cotangent):
    spot = lax.axis_index("row") * COLS + lax.axis_index("col")
    flag = (spot >= FIRST_DIAGONAL).astype(jnp.int32).reshape(1)
    head = jnp.pad(head_weight, ((0, 3), (0, 0)))
    bias = jnp.broadcast_to(jnp.pad(head_bias, (0, 3))[:, None], (40, 128))
    cot = jnp.pad(cotangent, ((0, CH - BINS), (0, 0), (0, 0)))

    packed = call(pack_kernel, [((DEVICES, 32, 128), BF16)], n=1)
    sent = jnp.concatenate(
        [packed(features.transpose(1, 0, 2))[0], packed(cot.transpose(1, 0, 2))[0]], axis=1
    )
    cells = exchange(sent)

    act1, stat, taps, sym = call(
        first_kernel, [FIELD, STAT, TAPS, BINH], [BINF, BINK, STACK], smem=1, n=2
    )(flag, cells, conv_first)
    table1 = exchange(stat)
    act2, stat, taps2 = call(second_kernel, [FIELD, STAT, TAPS], [STACK], n=3)(
        act1, table1, conv_second
    )
    table2 = exchange(stat)
    grad, stat, raw, term = call(third_kernel, [FIELD, STAT, BINF, ((40, 128), F32)], n=6)(
        act2, table2, taps, sym, head, bias
    )
    table3 = exchange(stat)
    grad1, stat, part2, logit = call(
        fourth_kernel, [FIELD, STAT, PART, BINH], [PADDED, TAPS, ACC, STACK, BINK, BINF], smem=1, n=10
    )(flag, act2, table2, grad, table3, taps2, act1, table1, conv_second, term, raw)
    table4 = exchange(stat)
    got2 = exchange(part2)
    part1, utaps = call(fifth_kernel, [PART, TAPS], [PADDED, ACC], n=5)(
        grad1, table4, act1, table1, taps
    )
    got1 = exchange(part1)
    result = exchange(
        call(sixth_kernel, [((DEVICES, 64, 128), BF16)], [HALF, STACK], n=4)(
            utaps, conv_first, grad, logit
        )[0]
    )
    summed = call(sum_kernel, [PART], n=1)
    all2 = exchange(summed(got2)[0])
    all1 = exchange(summed(got1)[0])
    unpacked = call(unpack_kernel, [HALF], n=1)
    input_grad = unpacked(result[:, :32])[0].transpose(1, 0, 2)
    logits = unpacked(result[:, 32:])[0].transpose(1, 0, 2)[:BINS]
    scale = 1.0 / 1024
    tail = all2[36:41].reshape(40, 128) * scale
    return (
        logits,
        input_grad,
        terms_of(all1) * scale,
        terms_of(all2) * scale,
        tail[:BINS, :CH],
        tail[:BINS, CH],
    )


def solution(mesh):
    placed = (P(None, "col", "row"), P(), P(), P(), P(), P(None, "col", "row"))
    return jax.shard_map(
        on_device,
        mesh=mesh,
        in_specs=placed,
        out_specs=(P(None, "col", "row"), P(None, "col", "row"), P(), P(), P(), P()),
        check_vma=False,
    )
```

```python
import jax
import jax.numpy as jnp
from jax import lax
from jax.experimental import pallas as pl
from jax.experimental.pallas import tpu as pltpu
from jax.sharding import PartitionSpec as P


STEP = 16
GRID = 64
epsilon = 1e-05
F32 = jnp.float32
BF16 = jnp.bfloat16
ROWS = 8
COLS = 16
DEVICES = 128
CH = 64
BINS = 37
CELLS = float(1024 * 1024)
OWN = float(64 * 128)
WIDE = 24
PARTS = 4


def class_table():
    place = {}
    count = 0
    for a in range(STEP):
        for b in range(a + 1, STEP):
            place[(a, b)] = (count, 0)
            place[(b, a)] = (count, 1)
            count += 1
    for a in range(STEP // 2):
        place[(a, a)] = (count, 0)
        place[(a + 8, a + 8)] = (count, 1)
        count += 1
    return place, STEP * (STEP - 1) // 2


PLACE, FIRST_DIAGONAL = class_table()


def dot(lhs, rhs):
    return jnp.dot(lhs, rhs, preferred_element_type=F32)


def dot_nt(lhs, rhs):
    return lax.dot_general(lhs, rhs, (((1,), (1,)), ((), ())), preferred_element_type=F32)


def iota(shape, dim):
    return lax.broadcasted_iota(jnp.int32, shape, dim)


def eye(n):
    return jnp.where(iota((n, n), 0) == iota((n, n), 1), 1.0, 0.0).astype(BF16)


def class_order():
    row = iota((128, 128), 0)
    lane = iota((128, 128), 1)
    return jnp.where(lane == STEP * (row % 8) + row // 8, 1.0, 0.0).astype(BF16)


def elu(z):
    return jnp.where(z > 0, z, jnp.exp(jnp.minimum(z, 0.0)) - 1.0)


def slope(z):
    return jnp.where(z > 0, 1.0, jnp.exp(jnp.minimum(z, 0.0)))


def pack_kernel(f_ref, c_ref, o_ref, f_s, c_s):
    order = class_order()
    f_s[...] = f_ref[...].astype(F32)
    c_s[0:BINS] = c_ref[...].astype(F32)
    c_s[BINS:40] = jnp.zeros((40 - BINS, GRID, 128), F32)
    pad = jnp.zeros((WIDE, 128), F32)

    def feature(j):
        return f_s[:, j, :]

    def bins(j):
        return jnp.concatenate([c_s[:, j, :], pad], axis=0)

    for first, get in ((0, feature), (32, bins)):
        for a in range(STEP):
            parts = []
            for h in range(2):
                x = jnp.concatenate([get(32 * h + a), get(32 * h + 16 + a)], axis=0)
                parts.append(dot_nt(order, x.astype(BF16)))
            for b in range(STEP):
                dest, slot = PLACE[(a, b)]
                tile = jnp.concatenate([p[8 * b : 8 * b + 8] for p in parts], axis=0)
                at = first + 16 * slot
                o_ref[dest, at : at + 16, :] = tile.astype(BF16)


def last_kernel(r_ref, f_ref, l_ref, first_ref, second_ref, head_ref, bias_ref, f_s, c_s):
    back = class_order()

    def feature(j, x):
        f_s[:, j, :] = x

    def bins(j, x):
        c_s[:, j, :] = x[:40]

    for first, put in ((0, feature), (32, bins)):
        for a in range(STEP):
            rows = [[], []]
            for b in range(STEP):
                src, slot = PLACE[(a, b)]
                at = first + 16 * slot
                tile = r_ref[src, at : at + 16, :].astype(F32)
                rows[0].append(tile[:8])
                rows[1].append(tile[8:])
            for h in range(2):
                z = jnp.concatenate(rows[h], axis=0)
                x = dot(z.T.astype(BF16), back)
                put(32 * h + a, x[:64])
                put(32 * h + 16 + a, x[64:])
    f_ref[...] = f_s[...].astype(BF16)
    l_ref[...] = c_s[0:BINS].astype(BF16)
    tail = r_ref[:, 64:72, :].astype(F32) * (1.0 / 1024)

    def fill(at, out_ref):
        low, mid, high = tail[:, at], tail[:, at + 1], tail[:, at + 2]
        left = jnp.concatenate([low, mid[:64]], axis=0)
        right = jnp.concatenate([mid[64:], high[:32]], axis=0)
        right = jnp.concatenate([right[:, :64], right[:, 64:]], axis=0)
        for kb in range(3):
            span = slice(64 * kb, 64 * kb + 64)
            out_ref[kb] = left[span, :64]
            out_ref[3 + kb] = left[span, 64:]
            out_ref[6 + kb] = right[span]
        return high

    fill(0, first_ref)
    high = fill(3, second_ref)
    head_ref[...] = high[32 : 32 + BINS, :64]
    bias_ref[...] = jnp.broadcast_to(high[:, 64:65], (128, 128)).T[0:1, 32 : 32 + BINS]


def collect(r_ref, first, put):
    unit = eye(128)

    def step(col, carry):
        rows = [[], []]
        for slot in range(2):
            for r in range(ROWS):
                tile = r_ref[r * COLS + col, first + 16 * slot : first + 16 * slot + 16, :].astype(F32)
                rows[0].append(tile[:8])
                rows[1].append(tile[8:])
        for h in range(2):
            z = jnp.concatenate(rows[h], axis=0).astype(BF16)
            t = dot_nt(unit, z)
            put(4 * col + 2 * h, t[:64])
            put(4 * col + 2 * h + 1, t[64:])
        return carry

    lax.fori_loop(0, COLS, step, 0)


def spread(o_ref, first, get):
    unit = eye(128)

    def step(col, carry):
        parts = []
        for h in range(2):
            y = jnp.concatenate([get(4 * col + 2 * h), get(4 * col + 2 * h + 1)], axis=0)
            parts.append(dot_nt(unit, y))
        for slot in range(2):
            for r in range(ROWS):
                at = 64 * slot + 8 * r
                tile = jnp.concatenate([p[at : at + 8] for p in parts], axis=0)
                o_ref[r * COLS + col, first + 16 * slot : first + 16 * slot + 16, :] = tile.astype(BF16)
        return carry

    lax.fori_loop(0, COLS, step, 0)


def put_taps(dst_ref, at, v):
    lane = iota((CH, 128), 1) % GRID
    dst_ref[at, 0:64, :] = jnp.where(lane == 0, 0.0, pltpu.roll(v, 1, 1)).astype(BF16)
    dst_ref[at, 64:128, :] = v.astype(BF16)
    dst_ref[at, 128:192, :] = jnp.where(lane == GRID - 1, 0.0, pltpu.roll(v, 127, 1)).astype(BF16)


def stack_weights(w_ref, dst_ref, adjoint):
    for kb in range(3):
        row = []
        for ka in range(3):
            if adjoint:
                row.append(w_ref[3 * (2 - ka) + (2 - kb)].astype(F32).T.astype(BF16))
            else:
                row.append(w_ref[3 * ka + kb])
        dst_ref[64 * kb : 64 * kb + 64, :] = jnp.concatenate(row, axis=1)


def convolve(w_ref, taps_ref, emit, state, before=None, after=None):
    w = w_ref[...]

    def step(t, carry):
        one, two, state = carry
        rhs = jnp.concatenate([taps_ref[2 * t], taps_ref[2 * t + 1]], axis=1)
        p = dot(w, rhs)
        a0, a1, a2 = p[0:64, :128], p[64:128, :128], p[128:192, :128]
        b0, b1, b2 = p[0:64, 128:], p[64:128, 128:], p[128:192, 128:]
        state = emit(2 * t - 1, one + a2, state)
        state = emit(2 * t, two + a1 + b2, state)
        return a0 + b1, b0, state

    zero = jnp.zeros((CH, 128), F32)
    carry = (zero, zero, state)
    for part in range(PARTS):
        if before is not None:
            before(part)
        carry = lax.fori_loop(8 * part, 8 * part + 8, step, carry)
        if part == PARTS - 1:
            one, two, state = carry
            state = emit(GRID - 1, one, state)
        if after is not None:
            after(part)
    return state


def whole(part):
    return slice(16 * part, 16 * part + 16)


def ready(part):
    first = 16 * part - 1 if part else 0
    last = 16 * part + 15 if part < PARTS - 1 else GRID
    return slice(first, last)


def copies(src, dst, sems, span=whole):
    return [
        pltpu.make_async_copy(src.at[span(part)], dst.at[span(part)], sems.at[part])
        for part in range(PARTS)
    ]


def start(*groups):
    for group in groups:
        for copy in group:
            copy.start()


def wait(*groups):
    for group in groups:
        for copy in group:
            copy.wait()


def weight_terms(u_ref, taps_ref, acc_ref):
    acc_ref[...] = jnp.zeros((192, 192), F32)

    def step(t, carry):
        lhs = []
        rhs = []
        for k in range(4):
            at = 4 * t + k
            lhs.append(jnp.concatenate([u_ref[at + 2], u_ref[at + 1], u_ref[at]], axis=0))
            rhs.append(taps_ref[at])
        acc_ref[...] += dot_nt(jnp.concatenate(lhs, axis=1), jnp.concatenate(rhs, axis=1))
        return carry

    lax.fori_loop(0, GRID // 4, step, 0)


def own_row(first, second):
    one = jnp.broadcast_to(jnp.sum(first, axis=1, keepdims=True), (CH, 128)).T
    two = jnp.broadcast_to(jnp.sum(second, axis=1, keepdims=True), (CH, 128)).T
    return jnp.concatenate([one[:, :64], two[:, :64]], axis=1)


def turned(row):
    return jnp.broadcast_to(row, (128, 128)).T


def moments(table_ref):
    table = table_ref[...]
    sums = jnp.sum(table, axis=0, keepdims=True)
    mean_row = sums / CELLS
    off = table / OWN - mean_row
    between = turned(OWN * jnp.sum(off * off, axis=0, keepdims=True))
    total = turned(sums)
    mean = total[:64] / CELLS
    spread_ = (total[64:] + between[:64]) / CELLS
    return mean, lax.rsqrt(spread_ + epsilon)


def means(table_ref):
    total = turned(jnp.sum(table_ref[...], axis=0, keepdims=True))
    return total[:64] / CELLS, total[64:] / CELLS


def own_moments(act_ref, total):
    mean = jnp.broadcast_to(jnp.sum(total, axis=1, keepdims=True) / OWN, (CH, 128))

    def step(j, acc):
        off = act_ref[j] - mean
        return acc + off * off

    square = lax.fori_loop(0, GRID, step, jnp.zeros((CH, 128), F32), unroll=4)
    return own_row(total, square)


def symmetric(x_ref, k_ref, flag):
    bins = x_ref.shape[1]
    k_ref[...] = jnp.swapaxes(x_ref[...], 0, 1)

    def step(k, carry):
        x = k_ref[k]
        t = x.T
        low, high = t[:64], t[64:]
        m = jnp.where(
            flag > 0,
            jnp.concatenate([low, high], axis=1),
            jnp.concatenate([high, low], axis=1),
        )
        k_ref[k] = 0.5 * (x + m)
        return carry

    lax.fori_loop(0, bins, step, 0, unroll=2)
    x_ref[...] = jnp.swapaxes(k_ref[...], 0, 1)


def first_kernel(r_hbm, w_ref, act_ref, stat_ref, taps_out, r_ref, taps_ref, w_s, sem, sem_out):
    cells = pltpu.make_async_copy(r_hbm.at[:, 0:32, :], r_ref, sem)
    cells.start()
    stack_weights(w_ref, w_s, False)
    cells.wait()

    def put(j, v):
        put_taps(taps_ref, j, v)

    collect(r_ref, 0, put)
    out = pltpu.make_async_copy(taps_ref, taps_out, sem_out)
    out.start()

    def emit(j, v, total):
        act_ref[jnp.maximum(j, 0)] = v
        return total + jnp.where(j >= 0, v, 0.0)

    total = convolve(w_s, taps_ref, emit, jnp.zeros((CH, 128), F32))
    stat_ref[...] = own_moments(act_ref, total)
    out.wait()


def sym_kernel(flag_ref, r_hbm, sym_ref, r_ref, x_ref, k_ref, sem):
    cells = pltpu.make_async_copy(r_hbm.at[:, 32:64, :], r_ref, sem)
    cells.start()
    cells.wait()

    def put(j, v):
        x_ref[j] = v[:40]

    collect(r_ref, 0, put)
    symmetric(x_ref, k_ref, flag_ref[0])
    sym_ref[...] = x_ref[...].astype(BF16)


def logit_kernel(flag_ref, raw_hbm, big_ref, x_ref, k_ref, o_ref, sem, sem_out):
    cells = pltpu.make_async_copy(raw_hbm, x_ref, sem)
    cells.start()
    cells.wait()
    symmetric(x_ref, k_ref, flag_ref[0])
    pad = jnp.zeros((WIDE, 128), F32)
    spread(o_ref, 0, lambda j: jnp.concatenate([x_ref[j], pad], axis=0).astype(BF16))
    out = pltpu.make_async_copy(o_ref, big_ref.at[:, 32:64, :], sem_out)
    out.start()
    out.wait()


def second_kernel(act_ref, table_ref, w_ref, out_hbm, stat_ref, taps_hbm, out_ref, taps_ref, w_s, sem_taps, sem_out):
    stack_weights(w_ref, w_s, False)
    mean, inverse = moments(table_ref)

    def step(j, carry):
        put_taps(taps_ref, j, elu((act_ref[j] - mean) * inverse))
        return carry

    lax.fori_loop(0, GRID, step, 0, unroll=2)
    taps_copy = pltpu.make_async_copy(taps_ref, taps_hbm, sem_taps)
    taps_copy.start()
    outs = copies(out_ref, out_hbm, sem_out, ready)

    def emit(j, v, total):
        out_ref[jnp.maximum(j, 0)] = v
        return total + jnp.where(j >= 0, v, 0.0)

    total = convolve(
        w_s, taps_ref, emit, jnp.zeros((CH, 128), F32), after=lambda part: outs[part].start()
    )
    stat_ref[...] = own_moments(out_ref, total)
    taps_copy.wait()
    wait(outs)


def third_kernel(
    act_hbm, table_ref, taps_hbm, sym_ref, head_ref, bias_ref,
    grad_hbm, stat_ref, raw_hbm, term_ref,
    act_ref, mid_ref, grad_ref, raw_ref, sem_act, sem_mid, sem_grad, sem_raw
):
    acts = copies(act_hbm, act_ref, sem_act)
    mids = [
        pltpu.make_async_copy(
            taps_hbm.at[whole(part), 64:128, :], mid_ref.at[whole(part)], sem_mid.at[part]
        )
        for part in range(PARTS)
    ]
    for part in range(PARTS):
        acts[part].start()
        mids[part].start()
    grads = copies(grad_ref, grad_hbm, sem_grad)
    raws = copies(raw_ref, raw_hbm, sem_raw)
    mean, inverse = moments(table_ref)
    head = head_ref[...]
    head_t = head.astype(F32).T.astype(BF16)
    bias = bias_ref[...]

    def step(j, carry):
        first, second, count, term = carry
        normed = (act_ref[j] - mean) * inverse
        summed = normed + mid_ref[j].astype(F32)
        hidden = elu(summed).astype(BF16)
        sym = sym_ref[j]
        raw_ref[j] = dot(head, hidden) + bias
        grad = dot(head_t, sym) * slope(summed)
        grad_ref[j] = grad
        term = term + dot_nt(sym, hidden)
        return first + grad, second + grad * normed, count + sym.astype(F32), term

    zero = jnp.zeros((CH, 128), F32)
    carry = (zero, zero, jnp.zeros((40, 128), F32), jnp.zeros((40, 64), F32))
    for part in range(PARTS):
        acts[part].wait()
        mids[part].wait()
        carry = lax.fori_loop(16 * part, 16 * part + 16, step, carry, unroll=2)
        grads[part].start()
        raws[part].start()
    first, second, count, term = carry
    stat_ref[...] = own_row(first, second)
    count = jnp.broadcast_to(jnp.sum(count, axis=1, keepdims=True), (40, 64))
    term_ref[...] = jnp.concatenate([term, count], axis=1)
    wait(grads, raws)


def store_terms(acc_ref, out_ref):
    acc = acc_ref[...]
    out_ref[0:192] = acc[:, :128]
    out_ref[192:288] = jnp.concatenate([acc[:96, 128:], acc[96:, 128:]], axis=1)


def norm_back(act_ref, moments_, grad_ref, means_, u_ref, utaps_ref, before):
    mean, inverse = moments_
    first_mean, second_mean = means_
    u_ref[0] = jnp.zeros((CH, 128), BF16)
    u_ref[GRID + 1] = jnp.zeros((CH, 128), BF16)

    def step(j, carry):
        normed = (act_ref[j] - mean) * inverse
        u = inverse * (grad_ref[j] - first_mean - normed * second_mean)
        u_ref[j + 1] = u.astype(BF16)
        put_taps(utaps_ref, j, u)
        return carry

    for part in range(PARTS):
        before(part)
        lax.fori_loop(16 * part, 16 * part + 16, step, 0, unroll=2)


def fourth_kernel(
    act_hbm, table_ref, grad_hbm, table3_ref, act1_ref, table1_ref, w_ref,
    out_hbm, stat_ref, u_hbm,
    act_ref, grad_ref, out_ref, u_ref, utaps_ref, w_s, sem_act, sem_grad, sem_out, sem_u
):
    acts = copies(act_hbm, act_ref, sem_act)
    grads = copies(grad_hbm, grad_ref, sem_grad)
    for part in range(PARTS):
        acts[part].start()
        grads[part].start()
    stack_weights(w_ref, w_s, True)

    def before(part):
        acts[part].wait()
        grads[part].wait()

    norm_back(act_ref, moments(table_ref), grad_ref, means(table3_ref), u_ref, utaps_ref, before)
    u_copy = pltpu.make_async_copy(u_ref, u_hbm, sem_u)
    u_copy.start()
    mean1, inverse1 = moments(table1_ref)
    outs = copies(out_ref, out_hbm, sem_out, ready)

    def emit(j, v, carry):
        first, second = carry
        at = jnp.maximum(j, 0)
        normed = (act1_ref[at] - mean1) * inverse1
        grad = jnp.where(j >= 0, v * slope(normed), 0.0)
        out_ref[at] = grad
        return first + grad, second + grad * normed

    zero = jnp.zeros((CH, 128), F32)
    first, second = convolve(
        w_s, utaps_ref, emit, (zero, zero), after=lambda part: outs[part].start()
    )
    stat_ref[...] = own_row(first, second)
    u_copy.wait()
    wait(outs)


def terms_kernel(u_hbm, taps_hbm, term_ref, out_ref, u_ref, taps_ref, acc_ref, sem_u, sem_taps):
    u_copy = pltpu.make_async_copy(u_hbm, u_ref, sem_u)
    u_copy.start()
    taps_copy = pltpu.make_async_copy(taps_hbm, taps_ref, sem_taps)
    taps_copy.start()
    u_copy.wait()
    taps_copy.wait()
    weight_terms(u_ref, taps_ref, acc_ref)
    store_terms(acc_ref, out_ref)
    out_ref[288:328] = term_ref[...]
    out_ref[328:384] = jnp.zeros((56, 128), F32)


def fifth_kernel(
    grad_hbm, table4_ref, act1_ref, table1_ref, taps_hbm, terms_ref,
    part_ref, utaps_hbm,
    grad_ref, taps_ref, utaps_ref, u_ref, acc_ref, buf_ref, sem_grad, sem_taps, sem_out
):
    grads = copies(grad_hbm, grad_ref, sem_grad)
    start(grads)
    taps_copy = pltpu.make_async_copy(taps_hbm, taps_ref, sem_taps)
    taps_copy.start()
    norm_back(
        act1_ref, moments(table1_ref), grad_ref, means(table4_ref), u_ref, utaps_ref,
        lambda part: grads[part].wait(),
    )
    out = pltpu.make_async_copy(utaps_ref, utaps_hbm, sem_out)
    out.start()
    taps_copy.wait()
    weight_terms(u_ref, taps_ref, acc_ref)
    store_terms(acc_ref, buf_ref)
    buf_ref[288:384] = jnp.zeros((96, 128), F32)
    for p in range(3):
        part_ref[:, p, :] = buf_ref[128 * p : 128 * p + 128]
        part_ref[:, 3 + p, :] = terms_ref[128 * p : 128 * p + 128]
    for p in range(6, 8):
        part_ref[:, p, :] = jnp.zeros((128, 128), F32)
    out.wait()


def sixth_kernel(
    utaps_hbm, w_ref, grad_hbm, big_in, big_ref,
    utaps_ref, grad_ref, x_ref, w_s, o_ref, sem_taps, sem_grad, sem_out
):
    taps = copies(utaps_hbm, utaps_ref, sem_taps)
    grads = copies(grad_hbm, grad_ref, sem_grad)
    for part in range(PARTS):
        taps[part].start()
        grads[part].start()
    stack_weights(w_ref, w_s, True)

    def before(part):
        taps[part].wait()
        grads[part].wait()

    def emit(j, v, carry):
        at = jnp.maximum(j, 0)
        x_ref[at] = (v + grad_ref[at]).astype(BF16)
        return carry

    convolve(w_s, utaps_ref, emit, 0, before=before)
    spread(o_ref, 0, lambda j: x_ref[j])
    out = pltpu.make_async_copy(o_ref, big_ref.at[:, 0:32, :], sem_out)
    out.start()
    out.wait()


def share_kernel(r_ref, big_in, big_ref, o_ref, sem):
    def step(k, acc):
        return acc + r_ref[k]

    total = lax.fori_loop(1, DEVICES, step, r_ref[0], unroll=8)
    o_ref[...] = jnp.broadcast_to(total.astype(BF16)[None], o_ref.shape)
    copy = pltpu.make_async_copy(o_ref, big_ref.at[:, 64:72, :], sem)
    copy.start()
    copy.wait()


def call(kernel, outs, ins, scratch=(), sems=(), alias=None, limit=28):
    spaces = {"v": pltpu.VMEM, "s": pltpu.SMEM, "h": pltpu.HBM}
    run = pl.pallas_call(
        kernel,
        out_shape=tuple(
            pltpu.HBM(o[0], o[1]) if len(o) > 2 else jax.ShapeDtypeStruct(o[0], o[1]) for o in outs
        ),
        in_specs=[pl.BlockSpec(memory_space=spaces[k]) for k in ins],
        out_specs=tuple(
            pl.BlockSpec(memory_space=pltpu.HBM if len(o) > 2 else pltpu.VMEM) for o in outs
        ),
        scratch_shapes=[pltpu.VMEM(o[0], o[1]) for o in scratch]
        + [pltpu.SemaphoreType.DMA((n,)) if n else pltpu.SemaphoreType.DMA for n in sems],
        input_output_aliases=alias or {},
        compiler_params=pltpu.CompilerParams(vmem_limit_bytes=limit << 20),
    )

    def placed(*args):
        return run(
            *(
                pltpu.with_memory_space_constraint(x, pltpu.HBM) if k == "h" else x
                for k, x in zip(ins, args)
            )
        )

    return placed


def hbm(form):
    return form + (True,)


def exchange(x):
    return lax.all_to_all(x, ("row", "col"), split_axis=0, concat_axis=0, tiled=True)


FIELD = ((GRID, CH, 128), F32)
HALF = ((GRID, CH, 128), BF16)
TAPS = ((GRID, 192, 128), BF16)
PADDED = ((GRID + 2, CH, 128), BF16)
STAT = ((128, 128), F32)
STACK = ((192, 192), BF16)
ACC = ((192, 192), F32)
PART = ((DEVICES, 8, 128), F32)
TERMS = ((384, 128), F32)
BIG = ((DEVICES, 72, 128), BF16)
PACKED = ((DEVICES, 32, 128), BF16)
PLANES = ((CH, GRID, 128), F32)
BINF = ((GRID, 40, 128), F32)
BINH = ((GRID, 40, 128), BF16)
BINK = ((40, GRID, 128), F32)


def on_device(features, conv_first, conv_second, head_weight, head_bias, cotangent):
    spot = lax.axis_index("row") * COLS + lax.axis_index("col")
    flag = (spot >= FIRST_DIAGONAL).astype(jnp.int32).reshape(1)
    head = jnp.pad(head_weight, ((0, 3), (0, 0)))
    bias = jnp.broadcast_to(jnp.pad(head_bias, (0, 3))[:, None], (40, 128))

    sent = call(pack_kernel, [((DEVICES, 64, 128), BF16)], "vv", [PLANES, BINK])(
        features, cotangent
    )[0]
    cells = exchange(sent)
    act1, stat, taps = call(
        first_kernel, [FIELD, STAT, hbm(TAPS)], "hv", [PACKED, TAPS, STACK], (0, 0)
    )(cells, conv_first)
    table1 = exchange(stat)
    sym = call(sym_kernel, [BINH], "sh", [PACKED, BINF, BINK], (0,))(flag, cells)[0]
    act2, stat, taps2 = call(
        second_kernel, [hbm(FIELD), STAT, hbm(TAPS)], "vvv", [FIELD, TAPS, STACK], (0, PARTS)
    )(act1, table1, conv_second)
    table2 = exchange(stat)
    table2, sym = lax.optimization_barrier((table2, sym))
    grad, stat, raw, term = call(
        third_kernel,
        [hbm(FIELD), STAT, hbm(BINF), ((40, 128), F32)],
        "hvhvvv",
        [FIELD, HALF, FIELD, BINF],
        (PARTS,) * 4,
    )(act2, table2, taps, sym, head, bias)
    table3 = exchange(stat)
    big = call(logit_kernel, [hbm(BIG)], "sh", [BINF, BINK, PACKED], (0, 0))(flag, raw)[0]
    table3, big = lax.optimization_barrier((table3, big))
    grad1, stat, u2 = call(
        fourth_kernel,
        [hbm(FIELD), STAT, hbm(PADDED)],
        "hvhvvvv",
        [FIELD, FIELD, FIELD, PADDED, TAPS, STACK],
        (PARTS, PARTS, PARTS, 0),
    )(act2, table2, grad, table3, act1, table1, conv_second)
    table4 = exchange(stat)
    terms2 = call(terms_kernel, [TERMS], "hhv", [PADDED, TAPS, ACC], (0, 0))(u2, taps2, term)[0]
    table4, terms2 = lax.optimization_barrier((table4, terms2))
    part, utaps = call(
        fifth_kernel,
        [PART, hbm(TAPS)],
        "hvvvhv",
        [FIELD, TAPS, TAPS, PADDED, ACC, TERMS],
        (PARTS, 0, 0),
    )(grad1, table4, act1, table1, taps, terms2)
    got = exchange(part)
    big = call(
        sixth_kernel,
        [hbm(BIG)],
        "hvhh",
        [TAPS, FIELD, HALF, STACK, PACKED],
        (PARTS, PARTS, 0),
        {3: 0},
    )(utaps, conv_first, grad, big)[0]
    big = call(share_kernel, [hbm(BIG)], "vh", [((DEVICES, 8, 128), BF16)], (0,), {1: 0})(got, big)[0]
    result = exchange(big)
    input_grad, logits, first, second, head_grad, bias_grad = call(
        last_kernel,
        [
            ((CH, GRID, 128), BF16),
            ((BINS, GRID, 128), BF16),
            ((9, CH, CH), F32),
            ((9, CH, CH), F32),
            ((BINS, CH), F32),
            ((1, BINS), F32),
        ],
        "v",
        [PLANES, BINK],
    )(result)
    return logits, input_grad, first, second, head_grad, bias_grad.reshape(BINS)


def solution(mesh):
    placed = (P(None, "col", "row"), P(), P(), P(), P(), P(None, "col", "row"))
    return jax.shard_map(
        on_device,
        mesh=mesh,
        in_specs=placed,
        out_specs=(P(None, "col", "row"), P(None, "col", "row"), P(), P(), P(), P()),
        check_vma=False,
    )
```

```python
import jax
import jax.numpy as jnp
from jax import lax
from jax.experimental import pallas as pl
from jax.experimental.pallas import tpu as pltpu
from jax.sharding import PartitionSpec as P


STEP = 16
GRID = 64
epsilon = 1e-05
F32 = jnp.float32
BF16 = jnp.bfloat16
ROWS = 8
COLS = 16
DEVICES = 128
CH = 64
BINS = 37
CELLS = float(1024 * 1024)
OWN = float(64 * 128)
WIDE = 24
PARTS = 4


def class_table():
    place = {}
    count = 0
    for a in range(STEP):
        for b in range(a + 1, STEP):
            place[(a, b)] = (count, 0)
            place[(b, a)] = (count, 1)
            count += 1
    for a in range(STEP // 2):
        place[(a, a)] = (count, 0)
        place[(a + 8, a + 8)] = (count, 1)
        count += 1
    return place, STEP * (STEP - 1) // 2


PLACE, FIRST_DIAGONAL = class_table()


def dot(lhs, rhs):
    return jnp.dot(lhs, rhs, preferred_element_type=F32)


def dot_nt(lhs, rhs):
    return lax.dot_general(lhs, rhs, (((1,), (1,)), ((), ())), preferred_element_type=F32)


def iota(shape, dim):
    return lax.broadcasted_iota(jnp.int32, shape, dim)


def eye(n):
    return jnp.where(iota((n, n), 0) == iota((n, n), 1), 1.0, 0.0).astype(BF16)


def class_order():
    row = iota((128, 128), 0)
    lane = iota((128, 128), 1)
    return jnp.where(lane == STEP * (row % 8) + row // 8, 1.0, 0.0).astype(BF16)


def elu(z):
    return jnp.where(z > 0, z, jnp.exp(jnp.minimum(z, 0.0)) - 1.0)


def slope(z):
    return jnp.where(z > 0, 1.0, jnp.exp(jnp.minimum(z, 0.0)))


def pack_kernel(f_ref, c_ref, o_ref, f_s, c_s):
    order = class_order()
    f_s[...] = f_ref[...].astype(F32)
    c_s[0:BINS] = c_ref[...].astype(F32)
    c_s[BINS:40] = jnp.zeros((40 - BINS, GRID, 128), F32)
    pad = jnp.zeros((WIDE, 128), F32)

    def feature(j):
        return f_s[:, j, :]

    def bins(j):
        return jnp.concatenate([c_s[:, j, :], pad], axis=0)

    for first, get in ((0, feature), (32, bins)):
        for a in range(STEP):
            parts = []
            for h in range(2):
                x = jnp.concatenate([get(32 * h + a), get(32 * h + 16 + a)], axis=0)
                parts.append(dot_nt(order, x.astype(BF16)))
            for b in range(STEP):
                dest, slot = PLACE[(a, b)]
                tile = jnp.concatenate([p[8 * b : 8 * b + 8] for p in parts], axis=0)
                at = first + 16 * slot
                o_ref[dest, at : at + 16, :] = tile.astype(BF16)


def last_kernel(r_ref, f_ref, l_ref, first_ref, second_ref, head_ref, bias_ref, f_s, c_s):
    back = class_order()

    def feature(j, x):
        f_s[:, j, :] = x

    def bins(j, x):
        c_s[:, j, :] = x[:40]

    for first, put in ((0, feature), (32, bins)):
        for a in range(STEP):
            rows = [[], []]
            for b in range(STEP):
                src, slot = PLACE[(a, b)]
                at = first + 16 * slot
                tile = r_ref[src, at : at + 16, :].astype(F32)
                rows[0].append(tile[:8])
                rows[1].append(tile[8:])
            for h in range(2):
                z = jnp.concatenate(rows[h], axis=0)
                x = dot(z.T.astype(BF16), back)
                put(32 * h + a, x[:64])
                put(32 * h + 16 + a, x[64:])
    f_ref[...] = f_s[...].astype(BF16)
    l_ref[...] = c_s[0:BINS].astype(BF16)
    tail = r_ref[:, 64:72, :].astype(F32) * (1.0 / 1024)

    def fill(at, out_ref):
        low, mid, high = tail[:, at], tail[:, at + 1], tail[:, at + 2]
        left = jnp.concatenate([low, mid[:64]], axis=0)
        right = jnp.concatenate([mid[64:], high[:32]], axis=0)
        right = jnp.concatenate([right[:, :64], right[:, 64:]], axis=0)
        for kb in range(3):
            span = slice(64 * kb, 64 * kb + 64)
            out_ref[kb] = left[span, :64]
            out_ref[3 + kb] = left[span, 64:]
            out_ref[6 + kb] = right[span]
        return high

    fill(0, first_ref)
    high = fill(3, second_ref)
    head_ref[...] = high[32 : 32 + BINS, :64]
    bias_ref[...] = jnp.broadcast_to(high[:, 64:65], (128, 128)).T[0:1, 32 : 32 + BINS]


def collect(r_ref, first, put):
    unit = eye(128)

    def step(col, carry):
        rows = [[], []]
        for slot in range(2):
            for r in range(ROWS):
                tile = r_ref[r * COLS + col, first + 16 * slot : first + 16 * slot + 16, :].astype(F32)
                rows[0].append(tile[:8])
                rows[1].append(tile[8:])
        for h in range(2):
            z = jnp.concatenate(rows[h], axis=0).astype(BF16)
            t = dot_nt(unit, z)
            put(4 * col + 2 * h, t[:64])
            put(4 * col + 2 * h + 1, t[64:])
        return carry

    lax.fori_loop(0, COLS, step, 0, unroll=8)


def spread(o_ref, first, get):
    unit = eye(128)

    def step(col, carry):
        parts = []
        for h in range(2):
            y = jnp.concatenate([get(4 * col + 2 * h), get(4 * col + 2 * h + 1)], axis=0)
            parts.append(dot_nt(unit, y))
        for slot in range(2):
            for r in range(ROWS):
                at = 64 * slot + 8 * r
                tile = jnp.concatenate([p[at : at + 8] for p in parts], axis=0)
                o_ref[r * COLS + col, first + 16 * slot : first + 16 * slot + 16, :] = tile.astype(BF16)
        return carry

    lax.fori_loop(0, COLS, step, 0, unroll=8)


def put_taps(dst_ref, at, v):
    lane = iota((CH, 128), 1) % GRID
    dst_ref[at, 0:64, :] = jnp.where(lane == 0, 0.0, pltpu.roll(v, 1, 1)).astype(BF16)
    dst_ref[at, 64:128, :] = v.astype(BF16)
    dst_ref[at, 128:192, :] = jnp.where(lane == GRID - 1, 0.0, pltpu.roll(v, 127, 1)).astype(BF16)


def stack_weights(w_ref, dst_ref, adjoint):
    for kb in range(3):
        row = []
        for ka in range(3):
            if adjoint:
                row.append(w_ref[3 * (2 - ka) + (2 - kb)].astype(F32).T.astype(BF16))
            else:
                row.append(w_ref[3 * ka + kb])
        dst_ref[64 * kb : 64 * kb + 64, :] = jnp.concatenate(row, axis=1)


def convolve(w_ref, taps_ref, emit, state, before=None, after=None):
    w = w_ref[...]

    def step(t, carry):
        one, two, state = carry
        rhs = jnp.concatenate([taps_ref[2 * t], taps_ref[2 * t + 1]], axis=1)
        p = dot(w, rhs)
        a0, a1, a2 = p[0:64, :128], p[64:128, :128], p[128:192, :128]
        b0, b1, b2 = p[0:64, 128:], p[64:128, 128:], p[128:192, 128:]
        state = emit(2 * t - 1, one + a2, state)
        state = emit(2 * t, two + a1 + b2, state)
        return a0 + b1, b0, state

    zero = jnp.zeros((CH, 128), F32)
    carry = (zero, zero, state)
    for part in range(PARTS):
        if before is not None:
            before(part)
        carry = lax.fori_loop(8 * part, 8 * part + 8, step, carry, unroll=8)
        if part == PARTS - 1:
            one, two, state = carry
            state = emit(GRID - 1, one, state)
        if after is not None:
            after(part)
    return state


def whole(part):
    return slice(16 * part, 16 * part + 16)


def ready(part):
    first = 16 * part - 1 if part else 0
    last = 16 * part + 15 if part < PARTS - 1 else GRID
    return slice(first, last)


def copies(src, dst, sems, span=whole):
    return [
        pltpu.make_async_copy(src.at[span(part)], dst.at[span(part)], sems.at[part])
        for part in range(PARTS)
    ]


def start(*groups):
    for group in groups:
        for copy in group:
            copy.start()


def wait(*groups):
    for group in groups:
        for copy in group:
            copy.wait()


def weight_terms(u_ref, taps_ref, acc_ref):
    acc_ref[...] = jnp.zeros((192, 192), F32)

    def step(t, carry):
        lhs = []
        rhs = []
        for k in range(4):
            at = 4 * t + k
            lhs.append(jnp.concatenate([u_ref[at + 2], u_ref[at + 1], u_ref[at]], axis=0))
            rhs.append(taps_ref[at])
        acc_ref[...] += dot_nt(jnp.concatenate(lhs, axis=1), jnp.concatenate(rhs, axis=1))
        return carry

    lax.fori_loop(0, GRID // 4, step, 0, unroll=8)


def own_row(first, second):
    one = jnp.broadcast_to(jnp.sum(first, axis=1, keepdims=True), (CH, 128)).T
    two = jnp.broadcast_to(jnp.sum(second, axis=1, keepdims=True), (CH, 128)).T
    return jnp.concatenate([one[:, :64], two[:, :64]], axis=1)


def turned(row):
    return jnp.broadcast_to(row, (128, 128)).T


def moments(table_ref):
    table = table_ref[...]
    sums = jnp.sum(table, axis=0, keepdims=True)
    mean_row = sums / CELLS
    off = table / OWN - mean_row
    between = turned(OWN * jnp.sum(off * off, axis=0, keepdims=True))
    total = turned(sums)
    mean = total[:64] / CELLS
    spread_ = (total[64:] + between[:64]) / CELLS
    return mean, lax.rsqrt(spread_ + epsilon)


def means(table_ref):
    total = turned(jnp.sum(table_ref[...], axis=0, keepdims=True))
    return total[:64] / CELLS, total[64:] / CELLS


def own_moments(act_ref, total):
    mean = jnp.broadcast_to(jnp.sum(total, axis=1, keepdims=True) / OWN, (CH, 128))

    def step(j, acc):
        off = act_ref[j] - mean
        return acc + off * off

    square = lax.fori_loop(0, GRID, step, jnp.zeros((CH, 128), F32), unroll=8)
    return own_row(total, square)


def symmetric(x_ref, k_ref, flag):
    bins = x_ref.shape[1]
    k_ref[...] = jnp.swapaxes(x_ref[...], 0, 1)

    def step(k, carry):
        x = k_ref[k]
        t = x.T
        low, high = t[:64], t[64:]
        m = jnp.where(
            flag > 0,
            jnp.concatenate([low, high], axis=1),
            jnp.concatenate([high, low], axis=1),
        )
        k_ref[k] = 0.5 * (x + m)
        return carry

    lax.fori_loop(0, bins, step, 0, unroll=8)
    x_ref[...] = jnp.swapaxes(k_ref[...], 0, 1)


def first_kernel(r_hbm, w_ref, act_ref, stat_ref, taps_out, r_ref, taps_ref, w_s, sem, sem_out):
    cells = pltpu.make_async_copy(r_hbm.at[:, 0:32, :], r_ref, sem)
    cells.start()
    stack_weights(w_ref, w_s, False)
    cells.wait()

    def put(j, v):
        put_taps(taps_ref, j, v)

    collect(r_ref, 0, put)
    out = pltpu.make_async_copy(taps_ref, taps_out, sem_out)
    out.start()

    def emit(j, v, total):
        act_ref[jnp.maximum(j, 0)] = v
        return total + jnp.where(j >= 0, v, 0.0)

    total = convolve(w_s, taps_ref, emit, jnp.zeros((CH, 128), F32))
    stat_ref[...] = own_moments(act_ref, total)
    out.wait()


def sym_kernel(flag_ref, r_hbm, sym_ref, r_ref, x_ref, k_ref, sem):
    cells = pltpu.make_async_copy(r_hbm.at[:, 32:64, :], r_ref, sem)
    cells.start()
    cells.wait()

    def put(j, v):
        x_ref[j] = v[:40]

    collect(r_ref, 0, put)
    symmetric(x_ref, k_ref, flag_ref[0])
    sym_ref[...] = x_ref[...].astype(BF16)


def logit_kernel(flag_ref, raw_hbm, big_ref, x_ref, k_ref, o_ref, sem, sem_out):
    cells = pltpu.make_async_copy(raw_hbm, x_ref, sem)
    cells.start()
    cells.wait()
    symmetric(x_ref, k_ref, flag_ref[0])
    pad = jnp.zeros((WIDE, 128), F32)
    spread(o_ref, 0, lambda j: jnp.concatenate([x_ref[j], pad], axis=0).astype(BF16))
    out = pltpu.make_async_copy(o_ref, big_ref.at[:, 32:64, :], sem_out)
    out.start()
    out.wait()


def second_kernel(act_ref, table_ref, w_ref, out_hbm, stat_ref, taps_hbm, out_ref, taps_ref, w_s, sem_taps, sem_out):
    stack_weights(w_ref, w_s, False)
    mean, inverse = moments(table_ref)

    def step(j, carry):
        put_taps(taps_ref, j, elu((act_ref[j] - mean) * inverse))
        return carry

    lax.fori_loop(0, GRID, step, 0, unroll=8)
    taps_copy = pltpu.make_async_copy(taps_ref, taps_hbm, sem_taps)
    taps_copy.start()
    outs = copies(out_ref, out_hbm, sem_out, ready)

    def emit(j, v, total):
        out_ref[jnp.maximum(j, 0)] = v
        return total + jnp.where(j >= 0, v, 0.0)

    total = convolve(
        w_s, taps_ref, emit, jnp.zeros((CH, 128), F32), after=lambda part: outs[part].start()
    )
    stat_ref[...] = own_moments(out_ref, total)
    taps_copy.wait()
    wait(outs)


def third_kernel(
    act_hbm, table_ref, taps_hbm, sym_ref, head_ref, bias_ref,
    grad_hbm, stat_ref, raw_hbm, term_ref,
    act_ref, mid_ref, grad_ref, raw_ref, sem_act, sem_mid, sem_grad, sem_raw
):
    acts = copies(act_hbm, act_ref, sem_act)
    mids = [
        pltpu.make_async_copy(
            taps_hbm.at[whole(part), 64:128, :], mid_ref.at[whole(part)], sem_mid.at[part]
        )
        for part in range(PARTS)
    ]
    for part in range(PARTS):
        acts[part].start()
        mids[part].start()
    grads = copies(grad_ref, grad_hbm, sem_grad)
    raws = copies(raw_ref, raw_hbm, sem_raw)
    mean, inverse = moments(table_ref)
    head = head_ref[...]
    head_t = head.astype(F32).T.astype(BF16)
    bias = bias_ref[...]

    wide = jnp.concatenate([bias, bias], axis=1)

    def step(t, carry):
        first, second, count, term = carry
        pair = (2 * t, 2 * t + 1)
        normed = [(act_ref[j] - mean) * inverse for j in pair]
        summed = [n + mid_ref[j].astype(F32) for n, j in zip(normed, pair)]
        hidden = jnp.concatenate([elu(x).astype(BF16) for x in summed], axis=1)
        sym = jnp.concatenate([sym_ref[j] for j in pair], axis=1)
        raw = dot(head, hidden) + wide
        back = dot(head_t, sym)
        term = term + dot_nt(sym, hidden)
        for k, j in enumerate(pair):
            raw_ref[j] = raw[:, 128 * k : 128 * k + 128]
            grad = back[:, 128 * k : 128 * k + 128] * slope(summed[k])
            grad_ref[j] = grad
            first = first + grad
            second = second + grad * normed[k]
            count = count + sym_ref[j].astype(F32)
        return first, second, count, term

    zero = jnp.zeros((CH, 128), F32)
    carry = (zero, zero, jnp.zeros((40, 128), F32), jnp.zeros((40, 64), F32))
    for part in range(PARTS):
        acts[part].wait()
        mids[part].wait()
        carry = lax.fori_loop(8 * part, 8 * part + 8, step, carry, unroll=8)
        grads[part].start()
        raws[part].start()
    first, second, count, term = carry
    stat_ref[...] = own_row(first, second)
    count = jnp.broadcast_to(jnp.sum(count, axis=1, keepdims=True), (40, 64))
    term_ref[...] = jnp.concatenate([term, count], axis=1)
    wait(grads, raws)


def store_terms(acc_ref, out_ref):
    acc = acc_ref[...]
    out_ref[0:192] = acc[:, :128]
    out_ref[192:288] = jnp.concatenate([acc[:96, 128:], acc[96:, 128:]], axis=1)


def norm_back(act_ref, moments_, grad_ref, means_, u_ref, utaps_ref, before):
    mean, inverse = moments_
    first_mean, second_mean = means_
    u_ref[0] = jnp.zeros((CH, 128), BF16)
    u_ref[GRID + 1] = jnp.zeros((CH, 128), BF16)

    def step(j, carry):
        normed = (act_ref[j] - mean) * inverse
        u = inverse * (grad_ref[j] - first_mean - normed * second_mean)
        u_ref[j + 1] = u.astype(BF16)
        put_taps(utaps_ref, j, u)
        return carry

    for part in range(PARTS):
        before(part)
        lax.fori_loop(16 * part, 16 * part + 16, step, 0, unroll=8)


def fourth_kernel(
    act_hbm, table_ref, grad_hbm, table3_ref, act1_ref, table1_ref, w_ref,
    out_hbm, stat_ref, u_hbm,
    act_ref, grad_ref, out_ref, u_ref, utaps_ref, w_s, sem_act, sem_grad, sem_out, sem_u
):
    acts = copies(act_hbm, act_ref, sem_act)
    grads = copies(grad_hbm, grad_ref, sem_grad)
    for part in range(PARTS):
        acts[part].start()
        grads[part].start()
    stack_weights(w_ref, w_s, True)

    def before(part):
        acts[part].wait()
        grads[part].wait()

    norm_back(act_ref, moments(table_ref), grad_ref, means(table3_ref), u_ref, utaps_ref, before)
    u_copy = pltpu.make_async_copy(u_ref, u_hbm, sem_u)
    u_copy.start()
    mean1, inverse1 = moments(table1_ref)
    outs = copies(out_ref, out_hbm, sem_out, ready)

    def emit(j, v, carry):
        first, second = carry
        at = jnp.maximum(j, 0)
        normed = (act1_ref[at] - mean1) * inverse1
        grad = jnp.where(j >= 0, v * slope(normed), 0.0)
        out_ref[at] = grad
        return first + grad, second + grad * normed

    zero = jnp.zeros((CH, 128), F32)
    first, second = convolve(
        w_s, utaps_ref, emit, (zero, zero), after=lambda part: outs[part].start()
    )
    stat_ref[...] = own_row(first, second)
    u_copy.wait()
    wait(outs)


def terms_kernel(u_hbm, taps_hbm, term_ref, out_ref, u_ref, taps_ref, acc_ref, sem_u, sem_taps):
    u_copy = pltpu.make_async_copy(u_hbm, u_ref, sem_u)
    u_copy.start()
    taps_copy = pltpu.make_async_copy(taps_hbm, taps_ref, sem_taps)
    taps_copy.start()
    u_copy.wait()
    taps_copy.wait()
    weight_terms(u_ref, taps_ref, acc_ref)
    store_terms(acc_ref, out_ref)
    out_ref[288:328] = term_ref[...]
    out_ref[328:384] = jnp.zeros((56, 128), F32)


def fifth_kernel(
    grad_hbm, table4_ref, act1_ref, table1_ref, taps_hbm, terms_ref,
    part_ref, utaps_hbm,
    grad_ref, taps_ref, utaps_ref, u_ref, acc_ref, buf_ref, sem_grad, sem_taps, sem_out
):
    grads = copies(grad_hbm, grad_ref, sem_grad)
    start(grads)
    taps_copy = pltpu.make_async_copy(taps_hbm, taps_ref, sem_taps)
    taps_copy.start()
    norm_back(
        act1_ref, moments(table1_ref), grad_ref, means(table4_ref), u_ref, utaps_ref,
        lambda part: grads[part].wait(),
    )
    out = pltpu.make_async_copy(utaps_ref, utaps_hbm, sem_out)
    out.start()
    taps_copy.wait()
    weight_terms(u_ref, taps_ref, acc_ref)
    store_terms(acc_ref, buf_ref)
    buf_ref[288:384] = jnp.zeros((96, 128), F32)
    for p in range(3):
        part_ref[:, p, :] = buf_ref[128 * p : 128 * p + 128]
        part_ref[:, 3 + p, :] = terms_ref[128 * p : 128 * p + 128]
    for p in range(6, 8):
        part_ref[:, p, :] = jnp.zeros((128, 128), F32)
    out.wait()


def sixth_kernel(
    utaps_hbm, w_ref, grad_hbm, big_in, big_ref,
    utaps_ref, grad_ref, x_ref, w_s, o_ref, sem_taps, sem_grad, sem_out
):
    taps = copies(utaps_hbm, utaps_ref, sem_taps)
    grads = copies(grad_hbm, grad_ref, sem_grad)
    for part in range(PARTS):
        taps[part].start()
        grads[part].start()
    stack_weights(w_ref, w_s, True)

    def before(part):
        taps[part].wait()
        grads[part].wait()

    def emit(j, v, carry):
        at = jnp.maximum(j, 0)
        x_ref[at] = (v + grad_ref[at]).astype(BF16)
        return carry

    convolve(w_s, utaps_ref, emit, 0, before=before)
    spread(o_ref, 0, lambda j: x_ref[j])
    out = pltpu.make_async_copy(o_ref, big_ref.at[:, 0:32, :], sem_out)
    out.start()
    out.wait()


def share_kernel(r_ref, big_in, big_ref, o_ref, sem):
    def step(k, acc):
        return acc + r_ref[k]

    total = lax.fori_loop(1, DEVICES, step, r_ref[0], unroll=8)
    o_ref[...] = jnp.broadcast_to(total.astype(BF16)[None], o_ref.shape)
    copy = pltpu.make_async_copy(o_ref, big_ref.at[:, 64:72, :], sem)
    copy.start()
    copy.wait()


def call(kernel, outs, ins, scratch=(), sems=(), alias=None, limit=28):
    spaces = {"v": pltpu.VMEM, "s": pltpu.SMEM, "h": pltpu.HBM}
    run = pl.pallas_call(
        kernel,
        out_shape=tuple(
            pltpu.HBM(o[0], o[1]) if len(o) > 2 else jax.ShapeDtypeStruct(o[0], o[1]) for o in outs
        ),
        in_specs=[pl.BlockSpec(memory_space=spaces[k]) for k in ins],
        out_specs=tuple(
            pl.BlockSpec(memory_space=pltpu.HBM if len(o) > 2 else pltpu.VMEM) for o in outs
        ),
        scratch_shapes=[pltpu.VMEM(o[0], o[1]) for o in scratch]
        + [pltpu.SemaphoreType.DMA((n,)) if n else pltpu.SemaphoreType.DMA for n in sems],
        input_output_aliases=alias or {},
        compiler_params=pltpu.CompilerParams(vmem_limit_bytes=limit << 20),
    )

    def placed(*args):
        return run(
            *(
                pltpu.with_memory_space_constraint(x, pltpu.HBM) if k == "h" else x
                for k, x in zip(ins, args)
            )
        )

    return placed


def hbm(form):
    return form + (True,)


def exchange(x):
    return lax.all_to_all(x, ("row", "col"), split_axis=0, concat_axis=0, tiled=True)


FIELD = ((GRID, CH, 128), F32)
HALF = ((GRID, CH, 128), BF16)
TAPS = ((GRID, 192, 128), BF16)
PADDED = ((GRID + 2, CH, 128), BF16)
STAT = ((128, 128), F32)
STACK = ((192, 192), BF16)
ACC = ((192, 192), F32)
PART = ((DEVICES, 8, 128), F32)
TERMS = ((384, 128), F32)
BIG = ((DEVICES, 72, 128), BF16)
PACKED = ((DEVICES, 32, 128), BF16)
PLANES = ((CH, GRID, 128), F32)
BINF = ((GRID, 40, 128), F32)
BINH = ((GRID, 40, 128), BF16)
BINK = ((40, GRID, 128), F32)


def on_device(features, conv_first, conv_second, head_weight, head_bias, cotangent):
    spot = lax.axis_index("row") * COLS + lax.axis_index("col")
    flag = (spot >= FIRST_DIAGONAL).astype(jnp.int32).reshape(1)
    head = jnp.pad(head_weight, ((0, 3), (0, 0)))
    bias = jnp.broadcast_to(jnp.pad(head_bias, (0, 3))[:, None], (40, 128))

    sent = call(pack_kernel, [((DEVICES, 64, 128), BF16)], "vv", [PLANES, BINK])(
        features, cotangent
    )[0]
    cells = exchange(sent)
    act1, stat, taps = call(
        first_kernel, [FIELD, STAT, hbm(TAPS)], "hv", [PACKED, TAPS, STACK], (0, 0)
    )(cells, conv_first)
    table1 = exchange(stat)
    sym = call(sym_kernel, [BINH], "sh", [PACKED, BINF, BINK], (0,))(flag, cells)[0]
    act2, stat, taps2 = call(
        second_kernel, [hbm(FIELD), STAT, hbm(TAPS)], "vvv", [FIELD, TAPS, STACK], (0, PARTS)
    )(act1, table1, conv_second)
    table2 = exchange(stat)
    table2, sym = lax.optimization_barrier((table2, sym))
    grad, stat, raw, term = call(
        third_kernel,
        [hbm(FIELD), STAT, hbm(BINF), ((40, 128), F32)],
        "hvhvvv",
        [FIELD, HALF, FIELD, BINF],
        (PARTS,) * 4,
    )(act2, table2, taps, sym, head, bias)
    table3 = exchange(stat)
    big = call(logit_kernel, [hbm(BIG)], "sh", [BINF, BINK, PACKED], (0, 0))(flag, raw)[0]
    table3, big = lax.optimization_barrier((table3, big))
    grad1, stat, u2 = call(
        fourth_kernel,
        [hbm(FIELD), STAT, hbm(PADDED)],
        "hvhvvvv",
        [FIELD, FIELD, FIELD, PADDED, TAPS, STACK],
        (PARTS, PARTS, PARTS, 0),
    )(act2, table2, grad, table3, act1, table1, conv_second)
    table4 = exchange(stat)
    terms2 = call(terms_kernel, [TERMS], "hhv", [PADDED, TAPS, ACC], (0, 0))(u2, taps2, term)[0]
    table4, terms2 = lax.optimization_barrier((table4, terms2))
    part, utaps = call(
        fifth_kernel,
        [PART, hbm(TAPS)],
        "hvvvhv",
        [FIELD, TAPS, TAPS, PADDED, ACC, TERMS],
        (PARTS, 0, 0),
    )(grad1, table4, act1, table1, taps, terms2)
    got = exchange(part)
    big = call(
        sixth_kernel,
        [hbm(BIG)],
        "hvhh",
        [TAPS, FIELD, HALF, STACK, PACKED],
        (PARTS, PARTS, 0),
        {3: 0},
    )(utaps, conv_first, grad, big)[0]
    big = call(share_kernel, [hbm(BIG)], "vh", [((DEVICES, 8, 128), BF16)], (0,), {1: 0})(got, big)[0]
    result = exchange(big)
    input_grad, logits, first, second, head_grad, bias_grad = call(
        last_kernel,
        [
            ((CH, GRID, 128), BF16),
            ((BINS, GRID, 128), BF16),
            ((9, CH, CH), F32),
            ((9, CH, CH), F32),
            ((BINS, CH), F32),
            ((1, BINS), F32),
        ],
        "v",
        [PLANES, BINK],
    )(result)
    return logits, input_grad, first, second, head_grad, bias_grad.reshape(BINS)


def solution(mesh):
    placed = (P(None, "col", "row"), P(), P(), P(), P(), P(None, "col", "row"))
    return jax.shard_map(
        on_device,
        mesh=mesh,
        in_specs=placed,
        out_specs=(P(None, "col", "row"), P(None, "col", "row"), P(), P(), P(), P()),
        check_vma=False,
    )
```

```python
import jax
import jax.numpy as jnp
from jax import lax
from jax.experimental import pallas as pl
from jax.experimental.pallas import tpu as pltpu
from jax.sharding import PartitionSpec as P


STEP = 16
GRID = 64
epsilon = 1e-05
F32 = jnp.float32
BF16 = jnp.bfloat16
ROWS = 8
COLS = 16
DEVICES = 128
CH = 64
BINS = 37
CELLS = float(1024 * 1024)
OWN = float(64 * 128)
PARTS = 4


def class_table():
    place = {}
    count = 0
    for a in range(STEP):
        for b in range(a + 1, STEP):
            place[(a, b)] = (count, 0)
            place[(b, a)] = (count, 1)
            count += 1
    for a in range(STEP // 2):
        place[(a, a)] = (count, 0)
        place[(a + 8, a + 8)] = (count, 1)
        count += 1
    return place, STEP * (STEP - 1) // 2


PLACE, FIRST_DIAGONAL = class_table()


def dot(lhs, rhs):
    return jnp.dot(lhs, rhs, preferred_element_type=F32)


def dot_nt(lhs, rhs):
    return lax.dot_general(lhs, rhs, (((1,), (1,)), ((), ())), preferred_element_type=F32)


def iota(shape, dim):
    return lax.broadcasted_iota(jnp.int32, shape, dim)


def eye(n):
    return jnp.where(iota((n, n), 0) == iota((n, n), 1), 1.0, 0.0).astype(BF16)


def class_order():
    row = iota((128, 128), 0)
    lane = iota((128, 128), 1)
    return jnp.where(lane == STEP * (row % 8) + row // 8, 1.0, 0.0).astype(BF16)


def elu(z):
    return jnp.where(z > 0, z, jnp.exp(jnp.minimum(z, 0.0)) - 1.0)


def slope(z):
    return jnp.where(z > 0, 1.0, jnp.exp(jnp.minimum(z, 0.0)))


def pack_kernel(f_ref, c_ref, o_ref, f_s, c_s):
    order = class_order()
    f_s[...] = f_ref[...].astype(F32)
    for a in range(STEP):
        parts = []
        for h in range(2):
            x = jnp.concatenate([f_s[:, 32 * h + a, :], f_s[:, 32 * h + 16 + a, :]], axis=0)
            parts.append(dot_nt(order, x.astype(BF16)))
        for b in range(STEP):
            dest, slot = PLACE[(a, b)]
            tile = jnp.concatenate([p[8 * b : 8 * b + 8] for p in parts], axis=0)
            o_ref[dest, 16 * slot : 16 * slot + 16, :] = tile.astype(BF16)
    c_s[0:BINS] = c_ref[...].astype(F32)
    c_s[BINS:40] = jnp.zeros((40 - BINS, GRID, 128), F32)
    o_ref[:, 48:56, :] = jnp.zeros((DEVICES, 8, 128), BF16)
    for a in range(STEP):
        bins = [c_s[:, 16 * low + a, :] for low in range(4)]
        x = jnp.concatenate([v[:32] for v in bins], axis=0)
        main = dot_nt(order, x.astype(BF16))
        x = jnp.concatenate([v[32:] for v in bins] * 2 + [jnp.zeros((64, 128), F32)], axis=0)
        rest = dot_nt(order, x.astype(BF16))
        for b in range(STEP):
            dest, slot = PLACE[(a, b)]
            span = slice(8 * b, 8 * b + 8)
            at = 32 + 8 * slot
            o_ref[dest, at : at + 8, :] = main[span].astype(BF16)
            lanes = slice(32 * slot, 32 * slot + 32)
            o_ref[dest, 48:56, lanes] = rest[span, lanes].astype(BF16)


def last_kernel(r_ref, f_ref, l_ref, first_ref, second_ref, head_ref, bias_ref, f_s, c_s):
    back = class_order()
    for a in range(STEP):
        rows = [[], []]
        for b in range(STEP):
            src, slot = PLACE[(a, b)]
            tile = r_ref[src, 16 * slot : 16 * slot + 16, :].astype(F32)
            rows[0].append(tile[:8])
            rows[1].append(tile[8:])
        for h in range(2):
            z = jnp.concatenate(rows[h], axis=0)
            x = dot(z.T.astype(BF16), back)
            f_s[:, 32 * h + a, :] = x[:64]
            f_s[:, 32 * h + 16 + a, :] = x[64:]
    f_ref[...] = f_s[...].astype(BF16)
    for a in range(STEP):
        main, rest = [], []
        for b in range(STEP):
            src, slot = PLACE[(a, b)]
            at = 32 + 8 * slot
            main.append(r_ref[src, at : at + 8, :].astype(F32))
            tile = r_ref[src, 48:56, :].astype(F32)
            rest.append(pltpu.roll(tile, 96, 1) if slot else tile)
        x = dot(jnp.concatenate(main, axis=0).T.astype(BF16), back)
        y = dot(jnp.concatenate(rest, axis=0).T[:32].astype(BF16), back)
        for low in range(4):
            c_s[0:32, 16 * low + a, :] = x[32 * low : 32 * low + 32]
            c_s[32:40, 16 * low + a, :] = y[8 * low : 8 * low + 8]
    l_ref[...] = c_s[0:BINS].astype(BF16)
    tail = r_ref[:, 56:64, :].astype(F32) * (1.0 / 1024)

    def fill(at, out_ref):
        low, mid, high = tail[:, at], tail[:, at + 1], tail[:, at + 2]
        left = jnp.concatenate([low, mid[:64]], axis=0)
        right = jnp.concatenate([mid[64:], high[:32]], axis=0)
        right = jnp.concatenate([right[:, :64], right[:, 64:]], axis=0)
        for kb in range(3):
            span = slice(64 * kb, 64 * kb + 64)
            out_ref[kb] = left[span, :64]
            out_ref[3 + kb] = left[span, 64:]
            out_ref[6 + kb] = right[span]
        return high

    fill(0, first_ref)
    high = fill(3, second_ref)
    head_ref[...] = high[32 : 32 + BINS, :64]
    bias_ref[...] = jnp.broadcast_to(high[:, 64:65], (128, 128)).T[0:1, 32 : 32 + BINS]


def collect(r_ref, first, put):
    unit = eye(128)

    def step(col, carry):
        rows = [[], []]
        for slot in range(2):
            for r in range(ROWS):
                tile = r_ref[r * COLS + col, first + 16 * slot : first + 16 * slot + 16, :].astype(F32)
                rows[0].append(tile[:8])
                rows[1].append(tile[8:])
        for h in range(2):
            z = jnp.concatenate(rows[h], axis=0).astype(BF16)
            t = dot_nt(unit, z)
            put(4 * col + 2 * h, t[:64])
            put(4 * col + 2 * h + 1, t[64:])
        return carry

    lax.fori_loop(0, COLS, step, 0, unroll=8)


def spread(o_ref, first, get):
    unit = eye(128)

    def step(col, carry):
        parts = []
        for h in range(2):
            y = jnp.concatenate([get(4 * col + 2 * h), get(4 * col + 2 * h + 1)], axis=0)
            parts.append(dot_nt(unit, y))
        for slot in range(2):
            for r in range(ROWS):
                at = 64 * slot + 8 * r
                tile = jnp.concatenate([p[at : at + 8] for p in parts], axis=0)
                o_ref[r * COLS + col, first + 16 * slot : first + 16 * slot + 16, :] = tile.astype(BF16)
        return carry

    lax.fori_loop(0, COLS, step, 0, unroll=8)


def collect_bins(r_ref, put):
    unit = eye(128)
    lane = iota((32, 128), 1)

    def step(col, carry):
        main = [
            r_ref[r * COLS + col, 8 * slot : 8 * slot + 8, :].astype(F32)
            for slot in range(2)
            for r in range(ROWS)
        ]
        rest = [r_ref[r * COLS + col, 16:24, :].astype(F32) for r in range(ROWS)] * 2
        x = dot_nt(unit, jnp.concatenate(main, axis=0).astype(BF16))
        y = dot_nt(unit, jnp.concatenate(rest, axis=0).astype(BF16))
        y = jnp.where(lane < 64, y[:32], y[32:64])
        for low in range(4):
            put(
                4 * col + low,
                jnp.concatenate([x[32 * low : 32 * low + 32], y[8 * low : 8 * low + 8]], axis=0),
            )
        return carry

    lax.fori_loop(0, COLS, step, 0, unroll=8)


def spread_bins(o_ref, get):
    unit = eye(128)
    lane = iota((8, 128), 1)

    def step(col, carry):
        bins = [get(4 * col + low) for low in range(4)]
        x = jnp.concatenate([v[:32] for v in bins], axis=0)
        main = dot_nt(unit, x.astype(BF16))
        x = jnp.concatenate([v[32:] for v in bins] * 2 + [jnp.zeros((64, 128), F32)], axis=0)
        rest = dot_nt(unit, x.astype(BF16))
        for r in range(ROWS):
            for slot in range(2):
                at = 64 * slot + 8 * r
                o_ref[r * COLS + col, 8 * slot : 8 * slot + 8, :] = main[at : at + 8].astype(BF16)
            tile = jnp.where(lane < 32, rest[8 * r : 8 * r + 8], rest[64 + 8 * r : 72 + 8 * r])
            o_ref[r * COLS + col, 16:24, :] = tile.astype(BF16)
        return carry

    lax.fori_loop(0, COLS, step, 0, unroll=8)


def put_taps(dst_ref, at, v):
    lane = iota((CH, 128), 1) % GRID
    dst_ref[at, 0:64, :] = jnp.where(lane == 0, 0.0, pltpu.roll(v, 1, 1)).astype(BF16)
    dst_ref[at, 64:128, :] = v.astype(BF16)
    dst_ref[at, 128:192, :] = jnp.where(lane == GRID - 1, 0.0, pltpu.roll(v, 127, 1)).astype(BF16)


def stack_weights(w_ref, dst_ref, adjoint):
    for kb in range(3):
        row = []
        for ka in range(3):
            if adjoint:
                row.append(w_ref[3 * (2 - ka) + (2 - kb)].astype(F32).T.astype(BF16))
            else:
                row.append(w_ref[3 * ka + kb])
        dst_ref[64 * kb : 64 * kb + 64, :] = jnp.concatenate(row, axis=1)


def convolve(w_ref, taps_ref, emit, state, before=None, after=None):
    w = w_ref[...]

    def step(t, carry):
        one, two, state = carry
        rhs = jnp.concatenate([taps_ref[2 * t], taps_ref[2 * t + 1]], axis=1)
        p = dot(w, rhs)
        a0, a1, a2 = p[0:64, :128], p[64:128, :128], p[128:192, :128]
        b0, b1, b2 = p[0:64, 128:], p[64:128, 128:], p[128:192, 128:]
        state = emit(2 * t - 1, one + a2, state)
        state = emit(2 * t, two + a1 + b2, state)
        return a0 + b1, b0, state

    zero = jnp.zeros((CH, 128), F32)
    carry = (zero, zero, state)
    for part in range(PARTS):
        if before is not None:
            before(part)
        carry = lax.fori_loop(8 * part, 8 * part + 8, step, carry, unroll=8)
        if part == PARTS - 1:
            one, two, state = carry
            state = emit(GRID - 1, one, state)
        if after is not None:
            after(part)
    return state


def whole(part):
    return slice(16 * part, 16 * part + 16)


def ready(part):
    first = 16 * part - 1 if part else 0
    last = 16 * part + 15 if part < PARTS - 1 else GRID
    return slice(first, last)


def copies(src, dst, sems, span=whole):
    return [
        pltpu.make_async_copy(src.at[span(part)], dst.at[span(part)], sems.at[part])
        for part in range(PARTS)
    ]


def start(*groups):
    for group in groups:
        for copy in group:
            copy.start()


def wait(*groups):
    for group in groups:
        for copy in group:
            copy.wait()


def weight_terms(u_ref, taps_ref, acc_ref):
    acc_ref[...] = jnp.zeros((192, 192), F32)

    def step(t, carry):
        lhs = []
        rhs = []
        for k in range(4):
            at = 4 * t + k
            lhs.append(jnp.concatenate([u_ref[at + 2], u_ref[at + 1], u_ref[at]], axis=0))
            rhs.append(taps_ref[at])
        acc_ref[...] += dot_nt(jnp.concatenate(lhs, axis=1), jnp.concatenate(rhs, axis=1))
        return carry

    lax.fori_loop(0, GRID // 4, step, 0, unroll=8)


def own_row(first, second):
    one = jnp.broadcast_to(jnp.sum(first, axis=1, keepdims=True), (CH, 128)).T
    two = jnp.broadcast_to(jnp.sum(second, axis=1, keepdims=True), (CH, 128)).T
    return jnp.concatenate([one[:, :64], two[:, :64]], axis=1)


def turned(row):
    return jnp.broadcast_to(row, (128, 128)).T


def moments(table_ref):
    table = table_ref[...]
    sums = jnp.sum(table, axis=0, keepdims=True)
    mean_row = sums / CELLS
    off = table / OWN - mean_row
    between = turned(OWN * jnp.sum(off * off, axis=0, keepdims=True))
    total = turned(sums)
    mean = total[:64] / CELLS
    spread_ = (total[64:] + between[:64]) / CELLS
    return mean, lax.rsqrt(spread_ + epsilon)


def means(table_ref):
    total = turned(jnp.sum(table_ref[...], axis=0, keepdims=True))
    return total[:64] / CELLS, total[64:] / CELLS


def own_moments(act_ref, total):
    mean = jnp.broadcast_to(jnp.sum(total, axis=1, keepdims=True) / OWN, (CH, 128))

    def step(j, acc):
        off = act_ref[j] - mean
        return acc + off * off

    square = lax.fori_loop(0, GRID, step, jnp.zeros((CH, 128), F32), unroll=8)
    return own_row(total, square)


def symmetric(x_ref, k_ref, flag):
    bins = x_ref.shape[1]
    k_ref[...] = jnp.swapaxes(x_ref[...], 0, 1)

    def step(k, carry):
        x = k_ref[k]
        t = x.T
        low, high = t[:64], t[64:]
        m = jnp.where(
            flag > 0,
            jnp.concatenate([low, high], axis=1),
            jnp.concatenate([high, low], axis=1),
        )
        k_ref[k] = 0.5 * (x + m)
        return carry

    lax.fori_loop(0, bins, step, 0, unroll=8)
    x_ref[...] = jnp.swapaxes(k_ref[...], 0, 1)


def first_kernel(r_hbm, w_ref, act_ref, stat_ref, taps_out, r_ref, taps_ref, w_s, sem, sem_out):
    cells = pltpu.make_async_copy(r_hbm.at[:, 0:32, :], r_ref, sem)
    cells.start()
    stack_weights(w_ref, w_s, False)
    cells.wait()

    def put(j, v):
        put_taps(taps_ref, j, v)

    collect(r_ref, 0, put)
    out = pltpu.make_async_copy(taps_ref.at[:, 64:128, :], taps_out, sem_out)
    out.start()

    def emit(j, v, total):
        act_ref[jnp.maximum(j, 0)] = v
        return total + jnp.where(j >= 0, v, 0.0)

    total = convolve(w_s, taps_ref, emit, jnp.zeros((CH, 128), F32))
    stat_ref[...] = own_moments(act_ref, total)
    out.wait()


def sym_kernel(flag_ref, r_hbm, sym_ref, r_ref, x_ref, k_ref, sem):
    cells = pltpu.make_async_copy(r_hbm.at[:, 32:56, :], r_ref, sem)
    cells.start()
    cells.wait()

    def put(j, v):
        x_ref[j] = v

    collect_bins(r_ref, put)
    symmetric(x_ref, k_ref, flag_ref[0])
    sym_ref[...] = x_ref[...].astype(BF16)


def logit_kernel(flag_ref, raw_hbm, big_ref, x_ref, k_ref, o_ref, sem, sem_out):
    cells = pltpu.make_async_copy(raw_hbm, x_ref, sem)
    cells.start()
    cells.wait()
    symmetric(x_ref, k_ref, flag_ref[0])
    spread_bins(o_ref, lambda j: x_ref[j])
    out = pltpu.make_async_copy(o_ref, big_ref.at[:, 32:56, :], sem_out)
    out.start()
    out.wait()


def second_kernel(act_ref, table_ref, w_ref, out_hbm, stat_ref, taps_hbm, out_ref, taps_ref, w_s, sem_taps, sem_out):
    stack_weights(w_ref, w_s, False)
    mean, inverse = moments(table_ref)

    def step(j, carry):
        put_taps(taps_ref, j, elu((act_ref[j] - mean) * inverse))
        return carry

    lax.fori_loop(0, GRID, step, 0, unroll=8)
    taps_copy = pltpu.make_async_copy(taps_ref.at[:, 64:128, :], taps_hbm, sem_taps)
    taps_copy.start()
    outs = copies(out_ref, out_hbm, sem_out, ready)

    def emit(j, v, total):
        out_ref[jnp.maximum(j, 0)] = v
        return total + jnp.where(j >= 0, v, 0.0)

    total = convolve(
        w_s, taps_ref, emit, jnp.zeros((CH, 128), F32), after=lambda part: outs[part].start()
    )
    stat_ref[...] = own_moments(out_ref, total)
    taps_copy.wait()
    wait(outs)


def third_kernel(
    act_hbm, table_ref, taps_hbm, sym_ref, head_ref, bias_ref,
    grad_hbm, stat_ref, raw_hbm, term_ref,
    act_ref, mid_ref, grad_ref, raw_ref, sem_act, sem_mid, sem_grad, sem_raw
):
    acts = copies(act_hbm, act_ref, sem_act)
    mids = copies(taps_hbm, mid_ref, sem_mid)
    for part in range(PARTS):
        acts[part].start()
        mids[part].start()
    grads = copies(grad_ref, grad_hbm, sem_grad)
    raws = copies(raw_ref, raw_hbm, sem_raw)
    mean, inverse = moments(table_ref)
    head = head_ref[...]
    head_t = head.astype(F32).T.astype(BF16)
    bias = bias_ref[...]

    wide = jnp.concatenate([bias, bias], axis=1)

    def step(t, carry):
        first, second, count, term = carry
        pair = (2 * t, 2 * t + 1)
        normed = [(act_ref[j] - mean) * inverse for j in pair]
        summed = [n + mid_ref[j].astype(F32) for n, j in zip(normed, pair)]
        hidden = jnp.concatenate([elu(x).astype(BF16) for x in summed], axis=1)
        sym = jnp.concatenate([sym_ref[j] for j in pair], axis=1)
        raw = dot(head, hidden) + wide
        back = dot(head_t, sym)
        term = term + dot_nt(sym, hidden)
        for k, j in enumerate(pair):
            raw_ref[j] = raw[:, 128 * k : 128 * k + 128]
            grad = back[:, 128 * k : 128 * k + 128] * slope(summed[k])
            grad_ref[j] = grad
            first = first + grad
            second = second + grad * normed[k]
            count = count + sym_ref[j].astype(F32)
        return first, second, count, term

    zero = jnp.zeros((CH, 128), F32)
    carry = (zero, zero, jnp.zeros((40, 128), F32), jnp.zeros((40, 64), F32))
    for part in range(PARTS):
        acts[part].wait()
        mids[part].wait()
        carry = lax.fori_loop(8 * part, 8 * part + 8, step, carry, unroll=8)
        grads[part].start()
        raws[part].start()
    first, second, count, term = carry
    stat_ref[...] = own_row(first, second)
    count = jnp.broadcast_to(jnp.sum(count, axis=1, keepdims=True), (40, 64))
    term_ref[...] = jnp.concatenate([term, count], axis=1)
    wait(grads, raws)


def store_terms(acc_ref, out_ref):
    acc = acc_ref[...]
    out_ref[0:192] = acc[:, :128]
    out_ref[192:288] = jnp.concatenate([acc[:96, 128:], acc[96:, 128:]], axis=1)


def norm_back(act_ref, moments_, grad_ref, means_, u_ref, utaps_ref, before):
    mean, inverse = moments_
    first_mean, second_mean = means_
    u_ref[0] = jnp.zeros((CH, 128), BF16)
    u_ref[GRID + 1] = jnp.zeros((CH, 128), BF16)

    def step(j, carry):
        normed = (act_ref[j] - mean) * inverse
        u = inverse * (grad_ref[j] - first_mean - normed * second_mean)
        u_ref[j + 1] = u.astype(BF16)
        if utaps_ref is not None:
            put_taps(utaps_ref, j, u)
        return carry

    for part in range(PARTS):
        before(part)
        lax.fori_loop(16 * part, 16 * part + 16, step, 0, unroll=8)


def fourth_kernel(
    act_hbm, table_ref, grad_hbm, table3_ref, act1_ref, table1_ref, w_ref,
    out_hbm, stat_ref, u_hbm,
    act_ref, grad_ref, out_ref, u_ref, utaps_ref, w_s, sem_act, sem_grad, sem_out, sem_u
):
    acts = copies(act_hbm, act_ref, sem_act)
    grads = copies(grad_hbm, grad_ref, sem_grad)
    for part in range(PARTS):
        acts[part].start()
        grads[part].start()
    stack_weights(w_ref, w_s, True)

    def before(part):
        acts[part].wait()
        grads[part].wait()

    norm_back(act_ref, moments(table_ref), grad_ref, means(table3_ref), u_ref, utaps_ref, before)
    u_copy = pltpu.make_async_copy(u_ref, u_hbm, sem_u)
    u_copy.start()
    mean1, inverse1 = moments(table1_ref)
    outs = copies(out_ref, out_hbm, sem_out, ready)

    def emit(j, v, carry):
        first, second = carry
        at = jnp.maximum(j, 0)
        normed = (act1_ref[at] - mean1) * inverse1
        grad = jnp.where(j >= 0, v * slope(normed), 0.0)
        out_ref[at] = grad
        return first + grad, second + grad * normed

    zero = jnp.zeros((CH, 128), F32)
    first, second = convolve(
        w_s, utaps_ref, emit, (zero, zero), after=lambda part: outs[part].start()
    )
    stat_ref[...] = own_row(first, second)
    u_copy.wait()
    wait(outs)


def all_taps(mid_ref, taps_ref, first, last):
    def step(j, carry):
        put_taps(taps_ref, j, mid_ref[j].astype(F32))
        return carry

    lax.fori_loop(first, last, step, 0, unroll=8)


def terms_kernel(u_hbm, taps_hbm, term_ref, out_ref, u_ref, mid_ref, taps_ref, acc_ref, sem_u, sem_taps):
    taps_copy = pltpu.make_async_copy(taps_hbm, mid_ref, sem_taps)
    taps_copy.start()
    u_copy = pltpu.make_async_copy(u_hbm, u_ref, sem_u)
    u_copy.start()
    taps_copy.wait()
    all_taps(mid_ref, taps_ref, 0, GRID)
    u_copy.wait()
    weight_terms(u_ref, taps_ref, acc_ref)
    store_terms(acc_ref, out_ref)
    out_ref[288:328] = term_ref[...]
    out_ref[328:384] = jnp.zeros((56, 128), F32)


def fifth_kernel(
    grad_hbm, table4_ref, act1_ref, table1_ref, taps_hbm, terms_ref,
    part_ref, u_hbm,
    grad_ref, mid_ref, taps_ref, u_ref, acc_ref, buf_ref, sem_grad, sem_taps, sem_out
):
    taps_copy = pltpu.make_async_copy(taps_hbm, mid_ref, sem_taps)
    taps_copy.start()
    grads = copies(grad_hbm, grad_ref, sem_grad)
    start(grads)
    taps_copy.wait()
    all_taps(mid_ref, taps_ref, 0, GRID)
    norm_back(
        act1_ref, moments(table1_ref), grad_ref, means(table4_ref), u_ref, None,
        lambda part: grads[part].wait(),
    )
    out = pltpu.make_async_copy(u_ref.at[1:65], u_hbm, sem_out)
    out.start()
    weight_terms(u_ref, taps_ref, acc_ref)
    store_terms(acc_ref, buf_ref)
    buf_ref[288:384] = jnp.zeros((96, 128), F32)
    for p in range(3):
        part_ref[:, p, :] = buf_ref[128 * p : 128 * p + 128]
        part_ref[:, 3 + p, :] = terms_ref[128 * p : 128 * p + 128]
    for p in range(6, 8):
        part_ref[:, p, :] = jnp.zeros((128, 128), F32)
    out.wait()


def sixth_kernel(
    u_hbm, w_ref, grad_hbm, big_in, big_ref,
    u_ref, utaps_ref, grad_ref, x_ref, w_s, o_ref, sem_u, sem_grad, sem_out
):
    us = copies(u_hbm, u_ref, sem_u)
    grads = copies(grad_hbm, grad_ref, sem_grad)
    for part in range(PARTS):
        us[part].start()
        grads[part].start()
    stack_weights(w_ref, w_s, True)

    def before(part):
        us[part].wait()
        all_taps(u_ref, utaps_ref, 16 * part, 16 * part + 16)
        grads[part].wait()

    def emit(j, v, carry):
        at = jnp.maximum(j, 0)
        x_ref[at] = (v + grad_ref[at]).astype(BF16)
        return carry

    convolve(w_s, utaps_ref, emit, 0, before=before)
    spread(o_ref, 0, lambda j: x_ref[j])
    out = pltpu.make_async_copy(o_ref, big_ref.at[:, 0:32, :], sem_out)
    out.start()
    out.wait()


def share_kernel(r_ref, big_in, big_ref, o_ref, sem):
    def step(k, acc):
        return acc + r_ref[k]

    total = lax.fori_loop(1, DEVICES, step, r_ref[0], unroll=8)
    o_ref[...] = jnp.broadcast_to(total.astype(BF16)[None], o_ref.shape)
    copy = pltpu.make_async_copy(o_ref, big_ref.at[:, 56:64, :], sem)
    copy.start()
    copy.wait()


def call(kernel, outs, ins, scratch=(), sems=(), alias=None, limit=28):
    spaces = {"v": pltpu.VMEM, "s": pltpu.SMEM, "h": pltpu.HBM}
    run = pl.pallas_call(
        kernel,
        out_shape=tuple(
            pltpu.HBM(o[0], o[1]) if len(o) > 2 else jax.ShapeDtypeStruct(o[0], o[1]) for o in outs
        ),
        in_specs=[pl.BlockSpec(memory_space=spaces[k]) for k in ins],
        out_specs=tuple(
            pl.BlockSpec(memory_space=pltpu.HBM if len(o) > 2 else pltpu.VMEM) for o in outs
        ),
        scratch_shapes=[pltpu.VMEM(o[0], o[1]) for o in scratch]
        + [pltpu.SemaphoreType.DMA((n,)) if n else pltpu.SemaphoreType.DMA for n in sems],
        input_output_aliases=alias or {},
        compiler_params=pltpu.CompilerParams(vmem_limit_bytes=limit << 20),
    )

    def placed(*args):
        return run(
            *(
                pltpu.with_memory_space_constraint(x, pltpu.HBM) if k == "h" else x
                for k, x in zip(ins, args)
            )
        )

    return placed


def hbm(form):
    return form + (True,)


def exchange(x):
    return lax.all_to_all(x, ("row", "col"), split_axis=0, concat_axis=0, tiled=True)


FIELD = ((GRID, CH, 128), F32)
HALF = ((GRID, CH, 128), BF16)
TAPS = ((GRID, 192, 128), BF16)
PADDED = ((GRID + 2, CH, 128), BF16)
STAT = ((128, 128), F32)
STACK = ((192, 192), BF16)
ACC = ((192, 192), F32)
PART = ((DEVICES, 8, 128), F32)
TERMS = ((384, 128), F32)
BIG = ((DEVICES, 64, 128), BF16)
PACKED_BINS = ((DEVICES, 24, 128), BF16)
PACKED = ((DEVICES, 32, 128), BF16)
PLANES = ((CH, GRID, 128), F32)
BINF = ((GRID, 40, 128), F32)
BINH = ((GRID, 40, 128), BF16)
BINK = ((40, GRID, 128), F32)


def on_device(features, conv_first, conv_second, head_weight, head_bias, cotangent):
    spot = lax.axis_index("row") * COLS + lax.axis_index("col")
    flag = (spot >= FIRST_DIAGONAL).astype(jnp.int32).reshape(1)
    head = jnp.pad(head_weight, ((0, 3), (0, 0)))
    bias = jnp.broadcast_to(jnp.pad(head_bias, (0, 3))[:, None], (40, 128))

    sent = call(pack_kernel, [((DEVICES, 56, 128), BF16)], "vv", [PLANES, BINK])(
        features, cotangent
    )[0]
    cells = exchange(sent)
    act1, stat, taps = call(
        first_kernel, [FIELD, STAT, hbm(HALF)], "hv", [PACKED, TAPS, STACK], (0, 0)
    )(cells, conv_first)
    table1 = exchange(stat)
    sym = call(sym_kernel, [BINH], "sh", [PACKED_BINS, BINF, BINK], (0,))(flag, cells)[0]
    act2, stat, taps2 = call(
        second_kernel, [hbm(FIELD), STAT, hbm(HALF)], "vvv", [FIELD, TAPS, STACK], (0, PARTS)
    )(act1, table1, conv_second)
    table2 = exchange(stat)
    table2, sym = lax.optimization_barrier((table2, sym))
    grad, stat, raw, term = call(
        third_kernel,
        [hbm(FIELD), STAT, hbm(BINF), ((40, 128), F32)],
        "hvhvvv",
        [FIELD, HALF, FIELD, BINF],
        (PARTS,) * 4,
    )(act2, table2, taps, sym, head, bias)
    table3 = exchange(stat)
    big = call(logit_kernel, [hbm(BIG)], "sh", [BINF, BINK, PACKED_BINS], (0, 0))(flag, raw)[0]
    table3, big = lax.optimization_barrier((table3, big))
    grad1, stat, u2 = call(
        fourth_kernel,
        [hbm(FIELD), STAT, hbm(PADDED)],
        "hvhvvvv",
        [FIELD, FIELD, FIELD, PADDED, TAPS, STACK],
        (PARTS, PARTS, PARTS, 0),
    )(act2, table2, grad, table3, act1, table1, conv_second)
    table4 = exchange(stat)
    terms2 = call(terms_kernel, [TERMS], "hhv", [PADDED, HALF, TAPS, ACC], (0, 0))(u2, taps2, term)[0]
    table4, terms2 = lax.optimization_barrier((table4, terms2))
    part, u1 = call(
        fifth_kernel,
        [PART, hbm(HALF)],
        "hvvvhv",
        [FIELD, HALF, TAPS, PADDED, ACC, TERMS],
        (PARTS, 0, 0),
    )(grad1, table4, act1, table1, taps, terms2)
    got = exchange(part)
    big = call(
        sixth_kernel,
        [hbm(BIG)],
        "hvhh",
        [HALF, TAPS, FIELD, HALF, STACK, PACKED],
        (PARTS, PARTS, 0),
        {3: 0},
    )(u1, conv_first, grad, big)[0]
    big = call(share_kernel, [hbm(BIG)], "vh", [((DEVICES, 8, 128), BF16)], (0,), {1: 0})(got, big)[0]
    result = exchange(big)
    input_grad, logits, first, second, head_grad, bias_grad = call(
        last_kernel,
        [
            ((CH, GRID, 128), BF16),
            ((BINS, GRID, 128), BF16),
            ((9, CH, CH), F32),
            ((9, CH, CH), F32),
            ((BINS, CH), F32),
            ((1, BINS), F32),
        ],
        "v",
        [PLANES, BINK],
    )(result)
    return logits, input_grad, first, second, head_grad, bias_grad.reshape(BINS)


def solution(mesh):
    placed = (P(None, "col", "row"), P(), P(), P(), P(), P(None, "col", "row"))
    return jax.shard_map(
        on_device,
        mesh=mesh,
        in_specs=placed,
        out_specs=(P(None, "col", "row"), P(None, "col", "row"), P(), P(), P(), P()),
        check_vma=False,
    )
```

```python
import jax
import jax.numpy as jnp
from jax import lax
from jax.experimental import pallas as pl
from jax.experimental.pallas import tpu as pltpu
from jax.sharding import PartitionSpec as P


STEP = 16
GRID = 64
epsilon = 1e-05
F32 = jnp.float32
BF16 = jnp.bfloat16
ROWS = 8
COLS = 16
DEVICES = 128
CH = 64
BINS = 37
CELLS = float(1024 * 1024)
OWN = float(64 * 128)
PARTS = 4


def class_table():
    place = {}
    count = 0
    for a in range(STEP):
        for b in range(a + 1, STEP):
            place[(a, b)] = (count, 0)
            place[(b, a)] = (count, 1)
            count += 1
    for a in range(STEP // 2):
        place[(a, a)] = (count, 0)
        place[(a + 8, a + 8)] = (count, 1)
        count += 1
    return place, STEP * (STEP - 1) // 2


PLACE, FIRST_DIAGONAL = class_table()


def dot(lhs, rhs):
    return jnp.dot(lhs, rhs, preferred_element_type=F32)


def dot_nt(lhs, rhs):
    return lax.dot_general(lhs, rhs, (((1,), (1,)), ((), ())), preferred_element_type=F32)


def iota(shape, dim):
    return lax.broadcasted_iota(jnp.int32, shape, dim)


def eye(n):
    return jnp.where(iota((n, n), 0) == iota((n, n), 1), 1.0, 0.0).astype(BF16)


def class_order():
    row = iota((128, 128), 0)
    lane = iota((128, 128), 1)
    return jnp.where(lane == STEP * (row % 8) + row // 8, 1.0, 0.0).astype(BF16)


def elu(z):
    return jnp.where(z > 0, z, jnp.exp(jnp.minimum(z, 0.0)) - 1.0)


def slope(z):
    return jnp.where(z > 0, 1.0, jnp.exp(jnp.minimum(z, 0.0)))


def pack_kernel(f_hbm, c_hbm, o_ref, f_ref, c_ref, f_s, c_s, sem_f, sem_c):
    f_copy = pltpu.make_async_copy(f_hbm, f_ref, sem_f)
    f_copy.start()
    c_copy = pltpu.make_async_copy(c_hbm, c_ref, sem_c)
    c_copy.start()
    order = class_order()
    o_ref[:, 48:56, :] = jnp.zeros((DEVICES, 8, 128), BF16)
    c_s[BINS:40] = jnp.zeros((40 - BINS, GRID, 128), F32)
    f_copy.wait()
    f_s[...] = f_ref[...].astype(F32)
    for a in range(STEP):
        parts = []
        for h in range(2):
            x = jnp.concatenate([f_s[:, 32 * h + a, :], f_s[:, 32 * h + 16 + a, :]], axis=0)
            parts.append(dot_nt(order, x.astype(BF16)))
        for b in range(STEP):
            dest, slot = PLACE[(a, b)]
            tile = jnp.concatenate([p[8 * b : 8 * b + 8] for p in parts], axis=0)
            o_ref[dest, 16 * slot : 16 * slot + 16, :] = tile.astype(BF16)
    c_copy.wait()
    c_s[0:BINS] = c_ref[...].astype(F32)
    for a in range(STEP):
        bins = [c_s[:, 16 * low + a, :] for low in range(4)]
        x = jnp.concatenate([v[:32] for v in bins], axis=0)
        main = dot_nt(order, x.astype(BF16))
        x = jnp.concatenate([v[32:] for v in bins] * 2 + [jnp.zeros((64, 128), F32)], axis=0)
        rest = dot_nt(order, x.astype(BF16))
        for b in range(STEP):
            dest, slot = PLACE[(a, b)]
            span = slice(8 * b, 8 * b + 8)
            at = 32 + 8 * slot
            o_ref[dest, at : at + 8, :] = main[span].astype(BF16)
            lanes = slice(32 * slot, 32 * slot + 32)
            o_ref[dest, 48:56, lanes] = rest[span, lanes].astype(BF16)


def last_kernel(
    r_ref, f_hbm, l_hbm, first_ref, second_ref, head_ref, bias_ref, f_ref, l_ref, f_s, c_s, sem_f, sem_l
):
    back = class_order()
    for a in range(STEP):
        rows = [[], []]
        for b in range(STEP):
            src, slot = PLACE[(a, b)]
            tile = r_ref[src, 16 * slot : 16 * slot + 16, :].astype(F32)
            rows[0].append(tile[:8])
            rows[1].append(tile[8:])
        for h in range(2):
            z = jnp.concatenate(rows[h], axis=0)
            x = dot(z.T.astype(BF16), back)
            f_s[:, 32 * h + a, :] = x[:64]
            f_s[:, 32 * h + 16 + a, :] = x[64:]
    f_ref[...] = f_s[...].astype(BF16)
    f_copy = pltpu.make_async_copy(f_ref, f_hbm, sem_f)
    f_copy.start()
    for a in range(STEP):
        main, rest = [], []
        for b in range(STEP):
            src, slot = PLACE[(a, b)]
            at = 32 + 8 * slot
            main.append(r_ref[src, at : at + 8, :].astype(F32))
            tile = r_ref[src, 48:56, :].astype(F32)
            rest.append(pltpu.roll(tile, 96, 1) if slot else tile)
        x = dot(jnp.concatenate(main, axis=0).T.astype(BF16), back)
        y = dot(jnp.concatenate(rest, axis=0).T[:32].astype(BF16), back)
        for low in range(4):
            c_s[0:32, 16 * low + a, :] = x[32 * low : 32 * low + 32]
            c_s[32:40, 16 * low + a, :] = y[8 * low : 8 * low + 8]
    l_ref[...] = c_s[0:BINS].astype(BF16)
    l_copy = pltpu.make_async_copy(l_ref, l_hbm, sem_l)
    l_copy.start()
    tail = r_ref[:, 56:64, :].astype(F32) * (1.0 / 1024)

    def fill(at, out_ref):
        low, mid, high = tail[:, at], tail[:, at + 1], tail[:, at + 2]
        left = jnp.concatenate([low, mid[:64]], axis=0)
        right = jnp.concatenate([mid[64:], high[:32]], axis=0)
        right = jnp.concatenate([right[:, :64], right[:, 64:]], axis=0)
        for kb in range(3):
            span = slice(64 * kb, 64 * kb + 64)
            out_ref[kb] = left[span, :64]
            out_ref[3 + kb] = left[span, 64:]
            out_ref[6 + kb] = right[span]
        return high

    fill(0, first_ref)
    high = fill(3, second_ref)
    head_ref[...] = high[32 : 32 + BINS, :64]
    bias_ref[...] = jnp.broadcast_to(high[:, 64:65], (128, 128)).T[0:1, 32 : 32 + BINS]
    f_copy.wait()
    l_copy.wait()


def collect(r_ref, first, put):
    unit = eye(128)

    def step(col, carry):
        rows = [[], []]
        for slot in range(2):
            for r in range(ROWS):
                tile = r_ref[r * COLS + col, first + 16 * slot : first + 16 * slot + 16, :].astype(F32)
                rows[0].append(tile[:8])
                rows[1].append(tile[8:])
        for h in range(2):
            z = jnp.concatenate(rows[h], axis=0).astype(BF16)
            t = dot_nt(unit, z)
            put(4 * col + 2 * h, t[:64])
            put(4 * col + 2 * h + 1, t[64:])
        return carry

    lax.fori_loop(0, COLS, step, 0, unroll=8)


def spread(o_ref, first, get):
    unit = eye(128)

    def step(col, carry):
        parts = []
        for h in range(2):
            y = jnp.concatenate([get(4 * col + 2 * h), get(4 * col + 2 * h + 1)], axis=0)
            parts.append(dot_nt(unit, y))
        for slot in range(2):
            for r in range(ROWS):
                at = 64 * slot + 8 * r
                tile = jnp.concatenate([p[at : at + 8] for p in parts], axis=0)
                o_ref[r * COLS + col, first + 16 * slot : first + 16 * slot + 16, :] = tile.astype(BF16)
        return carry

    lax.fori_loop(0, COLS, step, 0, unroll=8)


def collect_bins(r_ref, put):
    unit = eye(128)
    lane = iota((32, 128), 1)

    def step(col, carry):
        main = [
            r_ref[r * COLS + col, 8 * slot : 8 * slot + 8, :].astype(F32)
            for slot in range(2)
            for r in range(ROWS)
        ]
        rest = [r_ref[r * COLS + col, 16:24, :].astype(F32) for r in range(ROWS)] * 2
        x = dot_nt(unit, jnp.concatenate(main, axis=0).astype(BF16))
        y = dot_nt(unit, jnp.concatenate(rest, axis=0).astype(BF16))
        y = jnp.where(lane < 64, y[:32], y[32:64])
        for low in range(4):
            put(
                4 * col + low,
                jnp.concatenate([x[32 * low : 32 * low + 32], y[8 * low : 8 * low + 8]], axis=0),
            )
        return carry

    lax.fori_loop(0, COLS, step, 0, unroll=8)


def spread_bins(o_ref, get):
    unit = eye(128)
    lane = iota((8, 128), 1)

    def step(col, carry):
        bins = [get(4 * col + low) for low in range(4)]
        x = jnp.concatenate([v[:32] for v in bins], axis=0)
        main = dot_nt(unit, x.astype(BF16))
        x = jnp.concatenate([v[32:] for v in bins] * 2 + [jnp.zeros((64, 128), F32)], axis=0)
        rest = dot_nt(unit, x.astype(BF16))
        for r in range(ROWS):
            for slot in range(2):
                at = 64 * slot + 8 * r
                o_ref[r * COLS + col, 8 * slot : 8 * slot + 8, :] = main[at : at + 8].astype(BF16)
            tile = jnp.where(lane < 32, rest[8 * r : 8 * r + 8], rest[64 + 8 * r : 72 + 8 * r])
            o_ref[r * COLS + col, 16:24, :] = tile.astype(BF16)
        return carry

    lax.fori_loop(0, COLS, step, 0, unroll=8)


def put_taps(dst_ref, at, v):
    lane = iota((CH, 128), 1) % GRID
    dst_ref[at, 0:64, :] = jnp.where(lane == 0, 0.0, pltpu.roll(v, 1, 1)).astype(BF16)
    dst_ref[at, 64:128, :] = v.astype(BF16)
    dst_ref[at, 128:192, :] = jnp.where(lane == GRID - 1, 0.0, pltpu.roll(v, 127, 1)).astype(BF16)


def stack_weights(w_ref, dst_ref, adjoint):
    for kb in range(3):
        row = []
        for ka in range(3):
            if adjoint:
                row.append(w_ref[3 * (2 - ka) + (2 - kb)].astype(F32).T.astype(BF16))
            else:
                row.append(w_ref[3 * ka + kb])
        dst_ref[64 * kb : 64 * kb + 64, :] = jnp.concatenate(row, axis=1)


def convolve(w_ref, taps_ref, emit, state, before=None, after=None):
    w = w_ref[...]

    def step(t, carry):
        one, two, state = carry
        rhs = jnp.concatenate([taps_ref[2 * t], taps_ref[2 * t + 1]], axis=1)
        p = dot(w, rhs)
        a0, a1, a2 = p[0:64, :128], p[64:128, :128], p[128:192, :128]
        b0, b1, b2 = p[0:64, 128:], p[64:128, 128:], p[128:192, 128:]
        state = emit(2 * t - 1, one + a2, state)
        state = emit(2 * t, two + a1 + b2, state)
        return a0 + b1, b0, state

    zero = jnp.zeros((CH, 128), F32)
    carry = (zero, zero, state)
    for part in range(PARTS):
        if before is not None:
            before(part)
        carry = lax.fori_loop(8 * part, 8 * part + 8, step, carry, unroll=8)
        if part == PARTS - 1:
            one, two, state = carry
            state = emit(GRID - 1, one, state)
        if after is not None:
            after(part)
    return state


def whole(part):
    return slice(16 * part, 16 * part + 16)


def ready(part):
    first = 16 * part - 1 if part else 0
    last = 16 * part + 15 if part < PARTS - 1 else GRID
    return slice(first, last)


def copies(src, dst, sems, span=whole):
    return [
        pltpu.make_async_copy(src.at[span(part)], dst.at[span(part)], sems.at[part])
        for part in range(PARTS)
    ]


def start(*groups):
    for group in groups:
        for copy in group:
            copy.start()


def wait(*groups):
    for group in groups:
        for copy in group:
            copy.wait()


def weight_terms(u_ref, taps_ref, acc_ref):
    acc_ref[...] = jnp.zeros((192, 192), F32)

    def step(t, carry):
        lhs = []
        rhs = []
        for k in range(4):
            at = 4 * t + k
            lhs.append(jnp.concatenate([u_ref[at + 2], u_ref[at + 1], u_ref[at]], axis=0))
            rhs.append(taps_ref[at])
        acc_ref[...] += dot_nt(jnp.concatenate(lhs, axis=1), jnp.concatenate(rhs, axis=1))
        return carry

    lax.fori_loop(0, GRID // 4, step, 0, unroll=16)


def own_row(first, second):
    one = jnp.broadcast_to(jnp.sum(first, axis=1, keepdims=True), (CH, 128)).T
    two = jnp.broadcast_to(jnp.sum(second, axis=1, keepdims=True), (CH, 128)).T
    return jnp.concatenate([one[:, :64], two[:, :64]], axis=1)


def turned(row):
    return jnp.broadcast_to(row, (128, 128)).T


def moments(table_ref):
    table = table_ref[...]
    sums = jnp.sum(table, axis=0, keepdims=True)
    mean_row = sums / CELLS
    off = table / OWN - mean_row
    between = turned(OWN * jnp.sum(off * off, axis=0, keepdims=True))
    total = turned(sums)
    mean = total[:64] / CELLS
    spread_ = (total[64:] + between[:64]) / CELLS
    return mean, lax.rsqrt(spread_ + epsilon)


def means(table_ref):
    total = turned(jnp.sum(table_ref[...], axis=0, keepdims=True))
    return total[:64] / CELLS, total[64:] / CELLS


def own_moments(act_ref, total):
    mean = jnp.broadcast_to(jnp.sum(total, axis=1, keepdims=True) / OWN, (CH, 128))

    def step(j, acc):
        off = act_ref[j] - mean
        return acc + off * off

    square = lax.fori_loop(0, GRID, step, jnp.zeros((CH, 128), F32), unroll=16)
    return own_row(total, square)


def symmetric(x_ref, k_ref, flag):
    bins = x_ref.shape[1]
    k_ref[...] = jnp.swapaxes(x_ref[...], 0, 1)

    def step(k, carry):
        x = k_ref[k]
        t = x.T
        low, high = t[:64], t[64:]
        m = jnp.where(
            flag > 0,
            jnp.concatenate([low, high], axis=1),
            jnp.concatenate([high, low], axis=1),
        )
        k_ref[k] = 0.5 * (x + m)
        return carry

    lax.fori_loop(0, bins, step, 0, unroll=8)
    x_ref[...] = jnp.swapaxes(k_ref[...], 0, 1)


def first_kernel(r_hbm, w_ref, act_ref, stat_ref, taps_out, r_ref, taps_ref, w_s, sem, sem_out):
    cells = pltpu.make_async_copy(r_hbm.at[:, 0:32, :], r_ref, sem)
    cells.start()
    stack_weights(w_ref, w_s, False)
    cells.wait()

    def put(j, v):
        put_taps(taps_ref, j, v)

    collect(r_ref, 0, put)
    out = pltpu.make_async_copy(taps_ref.at[:, 64:128, :], taps_out, sem_out)
    out.start()

    def emit(j, v, total):
        act_ref[jnp.maximum(j, 0)] = v
        return total + jnp.where(j >= 0, v, 0.0)

    total = convolve(w_s, taps_ref, emit, jnp.zeros((CH, 128), F32))
    stat_ref[...] = own_moments(act_ref, total)
    out.wait()


def sym_kernel(flag_ref, r_hbm, sym_ref, r_ref, x_ref, k_ref, sem):
    cells = pltpu.make_async_copy(r_hbm.at[:, 32:56, :], r_ref, sem)
    cells.start()
    cells.wait()

    def put(j, v):
        x_ref[j] = v

    collect_bins(r_ref, put)
    symmetric(x_ref, k_ref, flag_ref[0])
    sym_ref[...] = x_ref[...].astype(BF16)


def logit_kernel(flag_ref, raw_hbm, big_ref, x_ref, k_ref, o_ref, sem, sem_out):
    cells = pltpu.make_async_copy(raw_hbm, x_ref, sem)
    cells.start()
    cells.wait()
    symmetric(x_ref, k_ref, flag_ref[0])
    spread_bins(o_ref, lambda j: x_ref[j])
    out = pltpu.make_async_copy(o_ref, big_ref.at[:, 32:56, :], sem_out)
    out.start()
    out.wait()


def second_kernel(act_ref, table_ref, w_ref, out_hbm, stat_ref, taps_hbm, out_ref, taps_ref, w_s, sem_taps, sem_out):
    stack_weights(w_ref, w_s, False)
    mean, inverse = moments(table_ref)

    def step(j, carry):
        put_taps(taps_ref, j, elu((act_ref[j] - mean) * inverse))
        return carry

    lax.fori_loop(0, GRID, step, 0, unroll=16)
    taps_copy = pltpu.make_async_copy(taps_ref.at[:, 64:128, :], taps_hbm, sem_taps)
    taps_copy.start()
    outs = copies(out_ref, out_hbm, sem_out, ready)

    def emit(j, v, total):
        out_ref[jnp.maximum(j, 0)] = v
        return total + jnp.where(j >= 0, v, 0.0)

    total = convolve(
        w_s, taps_ref, emit, jnp.zeros((CH, 128), F32), after=lambda part: outs[part].start()
    )
    stat_ref[...] = own_moments(out_ref, total)
    taps_copy.wait()
    wait(outs)


def third_kernel(
    act_hbm, table_ref, taps_hbm, sym_ref, head_ref, bias_ref,
    grad_hbm, stat_ref, raw_hbm, term_ref,
    act_ref, mid_ref, grad_ref, raw_ref, sem_act, sem_mid, sem_grad, sem_raw
):
    acts = copies(act_hbm, act_ref, sem_act)
    mids = copies(taps_hbm, mid_ref, sem_mid)
    for part in range(PARTS):
        acts[part].start()
        mids[part].start()
    grads = copies(grad_ref, grad_hbm, sem_grad)
    raws = copies(raw_ref, raw_hbm, sem_raw)
    mean, inverse = moments(table_ref)
    head = head_ref[...]
    head_t = head.astype(F32).T.astype(BF16)
    bias = bias_ref[...]

    wide = jnp.concatenate([bias, bias], axis=1)

    def step(t, carry):
        first, second, count, term = carry
        pair = (2 * t, 2 * t + 1)
        normed = [(act_ref[j] - mean) * inverse for j in pair]
        summed = [n + mid_ref[j].astype(F32) for n, j in zip(normed, pair)]
        hidden = jnp.concatenate([elu(x).astype(BF16) for x in summed], axis=1)
        sym = jnp.concatenate([sym_ref[j] for j in pair], axis=1)
        raw = dot(head, hidden) + wide
        back = dot(head_t, sym)
        term = term + dot_nt(sym, hidden)
        for k, j in enumerate(pair):
            raw_ref[j] = raw[:, 128 * k : 128 * k + 128]
            grad = back[:, 128 * k : 128 * k + 128] * slope(summed[k])
            grad_ref[j] = grad
            first = first + grad
            second = second + grad * normed[k]
            count = count + sym_ref[j].astype(F32)
        return first, second, count, term

    zero = jnp.zeros((CH, 128), F32)
    carry = (zero, zero, jnp.zeros((40, 128), F32), jnp.zeros((40, 64), F32))
    for part in range(PARTS):
        acts[part].wait()
        mids[part].wait()
        carry = lax.fori_loop(8 * part, 8 * part + 8, step, carry, unroll=8)
        grads[part].start()
        raws[part].start()
    first, second, count, term = carry
    stat_ref[...] = own_row(first, second)
    count = jnp.broadcast_to(jnp.sum(count, axis=1, keepdims=True), (40, 64))
    term_ref[...] = jnp.concatenate([term, count], axis=1)
    wait(grads, raws)


def store_terms(acc_ref, out_ref):
    acc = acc_ref[...]
    out_ref[0:192] = acc[:, :128]
    out_ref[192:288] = jnp.concatenate([acc[:96, 128:], acc[96:, 128:]], axis=1)


def norm_back(act_ref, moments_, grad_ref, means_, u_ref, utaps_ref, before):
    mean, inverse = moments_
    first_mean, second_mean = means_
    u_ref[0] = jnp.zeros((CH, 128), BF16)
    u_ref[GRID + 1] = jnp.zeros((CH, 128), BF16)

    def step(j, carry):
        normed = (act_ref[j] - mean) * inverse
        u = inverse * (grad_ref[j] - first_mean - normed * second_mean)
        u_ref[j + 1] = u.astype(BF16)
        if utaps_ref is not None:
            put_taps(utaps_ref, j, u)
        return carry

    for part in range(PARTS):
        before(part)
        lax.fori_loop(16 * part, 16 * part + 16, step, 0, unroll=16)


def fourth_kernel(
    act_hbm, table_ref, grad_hbm, table3_ref, act1_ref, table1_ref, w_ref,
    out_hbm, stat_ref, u_hbm,
    act_ref, grad_ref, out_ref, u_ref, utaps_ref, w_s, sem_act, sem_grad, sem_out, sem_u
):
    acts = copies(act_hbm, act_ref, sem_act)
    grads = copies(grad_hbm, grad_ref, sem_grad)
    for part in range(PARTS):
        acts[part].start()
        grads[part].start()
    stack_weights(w_ref, w_s, True)

    def before(part):
        acts[part].wait()
        grads[part].wait()

    norm_back(act_ref, moments(table_ref), grad_ref, means(table3_ref), u_ref, utaps_ref, before)
    u_copy = pltpu.make_async_copy(u_ref, u_hbm, sem_u)
    u_copy.start()
    mean1, inverse1 = moments(table1_ref)
    outs = copies(out_ref, out_hbm, sem_out, ready)

    def emit(j, v, carry):
        first, second = carry
        at = jnp.maximum(j, 0)
        normed = (act1_ref[at] - mean1) * inverse1
        grad = jnp.where(j >= 0, v * slope(normed), 0.0)
        out_ref[at] = grad
        return first + grad, second + grad * normed

    zero = jnp.zeros((CH, 128), F32)
    first, second = convolve(
        w_s, utaps_ref, emit, (zero, zero), after=lambda part: outs[part].start()
    )
    stat_ref[...] = own_row(first, second)
    u_copy.wait()
    wait(outs)


def all_taps(mid_ref, taps_ref, first, last):
    def step(j, carry):
        put_taps(taps_ref, j, mid_ref[j].astype(F32))
        return carry

    lax.fori_loop(first, last, step, 0, unroll=16)


def terms_kernel(u_hbm, taps_hbm, term_ref, out_ref, u_ref, mid_ref, taps_ref, acc_ref, sem_u, sem_taps):
    taps_copy = pltpu.make_async_copy(taps_hbm, mid_ref, sem_taps)
    taps_copy.start()
    u_copy = pltpu.make_async_copy(u_hbm, u_ref, sem_u)
    u_copy.start()
    taps_copy.wait()
    all_taps(mid_ref, taps_ref, 0, GRID)
    u_copy.wait()
    weight_terms(u_ref, taps_ref, acc_ref)
    store_terms(acc_ref, out_ref)
    out_ref[288:328] = term_ref[...]
    out_ref[328:384] = jnp.zeros((56, 128), F32)


def fifth_kernel(
    grad_hbm, table4_ref, act1_ref, table1_ref, taps_hbm, terms_ref,
    part_ref, u_hbm,
    grad_ref, mid_ref, taps_ref, u_ref, acc_ref, buf_ref, sem_grad, sem_taps, sem_out
):
    taps_copy = pltpu.make_async_copy(taps_hbm, mid_ref, sem_taps)
    taps_copy.start()
    grads = copies(grad_hbm, grad_ref, sem_grad)
    start(grads)
    for p in range(3):
        part_ref[:, 3 + p, :] = terms_ref[128 * p : 128 * p + 128]
    for p in range(6, 8):
        part_ref[:, p, :] = jnp.zeros((128, 128), F32)
    buf_ref[288:384] = jnp.zeros((96, 128), F32)
    taps_copy.wait()
    all_taps(mid_ref, taps_ref, 0, GRID)
    norm_back(
        act1_ref, moments(table1_ref), grad_ref, means(table4_ref), u_ref, None,
        lambda part: grads[part].wait(),
    )
    out = pltpu.make_async_copy(u_ref.at[1:65], u_hbm, sem_out)
    out.start()
    weight_terms(u_ref, taps_ref, acc_ref)
    store_terms(acc_ref, buf_ref)
    for p in range(3):
        part_ref[:, p, :] = buf_ref[128 * p : 128 * p + 128]
    out.wait()


def sixth_kernel(
    u_hbm, w_ref, grad_hbm, big_in, big_ref,
    u_ref, utaps_ref, grad_ref, x_ref, w_s, o_ref, sem_u, sem_grad, sem_out
):
    us = copies(u_hbm, u_ref, sem_u)
    grads = copies(grad_hbm, grad_ref, sem_grad)
    for part in range(PARTS):
        us[part].start()
        grads[part].start()
    stack_weights(w_ref, w_s, True)

    def before(part):
        us[part].wait()
        all_taps(u_ref, utaps_ref, 16 * part, 16 * part + 16)
        grads[part].wait()

    def emit(j, v, carry):
        at = jnp.maximum(j, 0)
        x_ref[at] = (v + grad_ref[at]).astype(BF16)
        return carry

    convolve(w_s, utaps_ref, emit, 0, before=before)
    spread(o_ref, 0, lambda j: x_ref[j])
    out = pltpu.make_async_copy(o_ref, big_ref.at[:, 0:32, :], sem_out)
    out.start()
    out.wait()


def share_kernel(r_ref, big_in, big_ref, o_ref, sem):
    def step(k, acc):
        return acc + r_ref[k]

    total = lax.fori_loop(1, DEVICES, step, r_ref[0], unroll=8)
    o_ref[...] = jnp.broadcast_to(total.astype(BF16)[None], o_ref.shape)
    copy = pltpu.make_async_copy(o_ref, big_ref.at[:, 56:64, :], sem)
    copy.start()
    copy.wait()


def call(kernel, outs, ins, scratch=(), sems=(), alias=None, limit=28):
    spaces = {"v": pltpu.VMEM, "s": pltpu.SMEM, "h": pltpu.HBM}
    run = pl.pallas_call(
        kernel,
        out_shape=tuple(
            pltpu.HBM(o[0], o[1]) if len(o) > 2 else jax.ShapeDtypeStruct(o[0], o[1]) for o in outs
        ),
        in_specs=[pl.BlockSpec(memory_space=spaces[k]) for k in ins],
        out_specs=tuple(
            pl.BlockSpec(memory_space=pltpu.HBM if len(o) > 2 else pltpu.VMEM) for o in outs
        ),
        scratch_shapes=[pltpu.VMEM(o[0], o[1]) for o in scratch]
        + [pltpu.SemaphoreType.DMA((n,)) if n else pltpu.SemaphoreType.DMA for n in sems],
        input_output_aliases=alias or {},
        compiler_params=pltpu.CompilerParams(vmem_limit_bytes=limit << 20),
    )

    def placed(*args):
        return run(
            *(
                pltpu.with_memory_space_constraint(x, pltpu.HBM) if k == "h" else x
                for k, x in zip(ins, args)
            )
        )

    return placed


def hbm(form):
    return form + (True,)


def exchange(x):
    return lax.all_to_all(x, ("row", "col"), split_axis=0, concat_axis=0, tiled=True)


FIELD = ((GRID, CH, 128), F32)
HALF = ((GRID, CH, 128), BF16)
TAPS = ((GRID, 192, 128), BF16)
PADDED = ((GRID + 2, CH, 128), BF16)
STAT = ((128, 128), F32)
STACK = ((192, 192), BF16)
ACC = ((192, 192), F32)
PART = ((DEVICES, 8, 128), F32)
TERMS = ((384, 128), F32)
BIG = ((DEVICES, 64, 128), BF16)
PACKED_BINS = ((DEVICES, 24, 128), BF16)
PACKED = ((DEVICES, 32, 128), BF16)
PLANES = ((CH, GRID, 128), F32)
CELLS_OUT = ((CH, GRID, 128), BF16)
BINS_OUT = ((BINS, GRID, 128), BF16)
BINF = ((GRID, 40, 128), F32)
BINH = ((GRID, 40, 128), BF16)
BINK = ((40, GRID, 128), F32)


def on_device(features, conv_first, conv_second, head_weight, head_bias, cotangent):
    spot = lax.axis_index("row") * COLS + lax.axis_index("col")
    flag = (spot >= FIRST_DIAGONAL).astype(jnp.int32).reshape(1)
    head = jnp.pad(head_weight, ((0, 3), (0, 0)))
    bias = jnp.broadcast_to(jnp.pad(head_bias, (0, 3))[:, None], (40, 128))

    sent = call(
        pack_kernel, [((DEVICES, 56, 128), BF16)], "hh", [CELLS_OUT, BINS_OUT, PLANES, BINK], (0, 0)
    )(features, cotangent)[0]
    cells = exchange(sent)
    act1, stat, taps = call(
        first_kernel, [FIELD, STAT, hbm(HALF)], "hv", [PACKED, TAPS, STACK], (0, 0)
    )(cells, conv_first)
    table1 = exchange(stat)
    sym = call(sym_kernel, [BINH], "sh", [PACKED_BINS, BINF, BINK], (0,))(flag, cells)[0]
    act2, stat, taps2 = call(
        second_kernel, [hbm(FIELD), STAT, hbm(HALF)], "vvv", [FIELD, TAPS, STACK], (0, PARTS)
    )(act1, table1, conv_second)
    table2 = exchange(stat)
    table2, sym = lax.optimization_barrier((table2, sym))
    grad, stat, raw, term = call(
        third_kernel,
        [hbm(FIELD), STAT, hbm(BINF), ((40, 128), F32)],
        "hvhvvv",
        [FIELD, HALF, FIELD, BINF],
        (PARTS,) * 4,
    )(act2, table2, taps, sym, head, bias)
    table3 = exchange(stat)
    big = call(logit_kernel, [hbm(BIG)], "sh", [BINF, BINK, PACKED_BINS], (0, 0))(flag, raw)[0]
    table3, big = lax.optimization_barrier((table3, big))
    grad1, stat, u2 = call(
        fourth_kernel,
        [hbm(FIELD), STAT, hbm(PADDED)],
        "hvhvvvv",
        [FIELD, FIELD, FIELD, PADDED, TAPS, STACK],
        (PARTS, PARTS, PARTS, 0),
    )(act2, table2, grad, table3, act1, table1, conv_second)
    table4 = exchange(stat)
    terms2 = call(terms_kernel, [TERMS], "hhv", [PADDED, HALF, TAPS, ACC], (0, 0))(u2, taps2, term)[0]
    table4, terms2 = lax.optimization_barrier((table4, terms2))
    part, u1 = call(
        fifth_kernel,
        [PART, hbm(HALF)],
        "hvvvhv",
        [FIELD, HALF, TAPS, PADDED, ACC, TERMS],
        (PARTS, 0, 0),
    )(grad1, table4, act1, table1, taps, terms2)
    got = exchange(part)
    big = call(
        sixth_kernel,
        [hbm(BIG)],
        "hvhh",
        [HALF, TAPS, FIELD, HALF, STACK, PACKED],
        (PARTS, PARTS, 0),
        {3: 0},
    )(u1, conv_first, grad, big)[0]
    big = call(share_kernel, [hbm(BIG)], "vh", [((DEVICES, 8, 128), BF16)], (0,), {1: 0})(got, big)[0]
    result = exchange(big)
    input_grad, logits, first, second, head_grad, bias_grad = call(
        last_kernel,
        [
            hbm(CELLS_OUT),
            hbm(BINS_OUT),
            ((9, CH, CH), F32),
            ((9, CH, CH), F32),
            ((BINS, CH), F32),
            ((1, BINS), F32),
        ],
        "v",
        [CELLS_OUT, BINS_OUT, PLANES, BINK],
        (0, 0),
    )(result)
    return logits, input_grad, first, second, head_grad, bias_grad.reshape(BINS)


def solution(mesh):
    placed = (P(None, "col", "row"), P(), P(), P(), P(), P(None, "col", "row"))
    return jax.shard_map(
        on_device,
        mesh=mesh,
        in_specs=placed,
        out_specs=(P(None, "col", "row"), P(None, "col", "row"), P(), P(), P(), P()),
        check_vma=False,
    )
```
